256 devices in a mesh: param: 32 (over y, z_hi, core), tm: 8 (over z_lo, x).
Axes of the slice: x: 4, y: 4, z: 8 (z_hi: 4, z_lo: 2; z = z_hi * 2 + z_lo), core: 2. Of those that a mesh axis runs over, the one named last changes fastest.
Arguments:
- params: bfloat16 [32, 128, 16384], P(None, 'tm', 'param'), may hold values from -6 to 6
- kernel: bfloat16 [8, 16384, 600], P(None, 'param'), may hold values from -0.015625 to 0.015625
- lag_offsets: int32 [8], replicated, may hold values from 0 to 11, as said below
- observed: bfloat16 [32, 128, 600], P(None, 'tm'), may hold values from -6 to 6
- diag_inverse: float32 [600, 600], replicated, may hold values from -2 to 2, as said below
- coupling: float32 [3, 600, 600], replicated, may hold values from -26 to 26
Outputs:
- whitened: float32 [32, 128, 600], P(None, 'tm')
The draws below stay inside these ranges and needn't reach their ends.
Inputs may be any that keep to these rules, and one draw needn't show every extreme that they name: `lag_offsets`: the offsets are distinct and one of them is always 12 - 1. `diag_inverse`: lower triangular with a positive diagonal.
All inputs are finite; a program needn't handle non-finite values.
Results may differ from the reference program's by a relative error of at most 0.0003.
Values may be sent and summed in bfloat16 or wider, within the bound.
No kernel may reach another device: no remote copies, remote signals or barrier semaphores. Data moves between devices by JAX's collectives and lax.ppermute only.
A program may use at most 64 MiB of HBM per device.

```python
import math
import jax
import jax.numpy as jnp
from jax import lax

SENSORS = 600
LAGS = 8
REACH = 12
BAND = 4
SAMPLES = 32
PCOLS = 16384
STEPS = 128


def draw_lag_offsets(key, part):
    chosen = jax.random.permutation(key, REACH - 1)[:LAGS - 1]
    return jnp.concatenate([chosen, jnp.array([REACH - 1])]).astype(jnp.int32)


def noise_parts(key):
    keys = jax.random.split(jax.random.fold_in(key, 7), 4)
    count = SENSORS
    scales = jax.random.uniform(keys[0], (count,), jnp.float32, 0.05, 0.1)
    lower = jax.random.normal(keys[1], (count, count), jnp.float32) * (0.4 * 0.075 / count ** 0.5)
    rate_log = jax.random.uniform(keys[2], (count,), jnp.float32, math.log(0.5 / STEPS), math.log(1.0 / 15.0))
    retention = jnp.exp(-jnp.exp(rate_log))
    inverse_block = jnp.tril(lower, -1) + jnp.diag(scales)
    factor = jnp.linalg.solve(inverse_block, jnp.eye(count, dtype=jnp.float32))
    mixing = jax.random.normal(keys[3], (BAND - 1, count, count), jnp.float32) * (0.0025 / count ** 0.5)
    leading = mixing[0] - jnp.diag(retention)
    stacked = jnp.concatenate([leading[None], mixing[1:]], axis=0)
    coupled = jnp.einsum('mn,jnk->jmk', factor, stacked, precision=lax.Precision.HIGHEST)
    return (inverse_block.astype(jnp.float32), coupled.astype(jnp.float32))


def draw_diag_inverse(key, part):
    inverse_block, coupled = noise_parts(key)
    return inverse_block


def draw_coupling(key, part):
    inverse_block, coupled = noise_parts(key)
    return coupled


def shard_levels(rng, dims, shards, low, largest):
    gain, own = 1.0, jax.random.fold_in(rng, 6)
    for position, shards_of in shards:
        draws = jnp.exp(jax.random.uniform(jax.random.fold_in(own, position), (shards_of,), jnp.float32, low / len(shards), largest / len(shards)))
        gain = gain * jnp.repeat(draws, dims[position] // shards_of).reshape([-1 if axis == position else 1 for axis in range(len(dims))])
    return gain


def gaussian(own_key, extent, scale, reach, pieces=(), held_as=jnp.bfloat16):
    values = scale * jax.random.normal(own_key, extent, jnp.float32)
    if pieces:
        values = values * shard_levels(own_key, extent, pieces, -0.22, 0.18)
    return jnp.clip(values, -reach, reach).astype(held_as)


def setup_inputs(seed: int = 0) -> dict:
    splits = jax.random.split(jax.random.key(seed), 7)
    return {
        "params": gaussian(splits[0], (SAMPLES, STEPS, PCOLS), 1.0, 6.0, ((1, 8), (2, 32))),
        "kernel": gaussian(splits[1], (LAGS, PCOLS, SENSORS), (LAGS * PCOLS) ** -0.5, 0.015625, ((1, 32),)),
        "lag_offsets": draw_lag_offsets(jax.random.fold_in(splits[6], 71), 0),
        "observed": gaussian(splits[3], (SAMPLES, STEPS, SENSORS), 1.0, 6.0, ((1, 8),)),
        "diag_inverse": draw_diag_inverse(jax.random.fold_in(splits[6], 71), 0),
        "coupling": draw_coupling(jax.random.fold_in(splits[6], 71), 0),
    }


def reference(params, kernel, lag_offsets, observed, diag_inverse, coupling):
    padded = jnp.pad(params, ((0, 0), (REACH - 1, 0), (0, 0)))
    predicted = jnp.zeros((SAMPLES, STEPS, SENSORS), jnp.float32)
    for lag_index in range(LAGS):
        start = (REACH - 1 - lag_offsets[lag_index]).astype(jnp.int32)
        window = lax.dynamic_slice_in_dim(padded, start, STEPS, 1)
        term = jnp.dot(window.reshape(SAMPLES * STEPS, PCOLS).astype(jnp.float32), kernel[lag_index].astype(jnp.float32), preferred_element_type=jnp.float32)
        predicted = predicted + term.reshape(SAMPLES, STEPS, SENSORS)
    misfit = observed.astype(jnp.float32) - predicted

    def advance(history, current):
        balance = current - jnp.einsum('jsn,jmn->sm', history, coupling, precision=lax.Precision.HIGHEST)
        solved = jnp.dot(balance, diag_inverse.T, precision=lax.Precision.HIGHEST)
        history = jnp.concatenate([solved[None], history[:-1]], axis=0)
        return (history, solved)
    start_history = jnp.zeros((BAND - 1, SAMPLES, SENSORS), jnp.float32)
    final_history, solved_all = lax.scan(advance, start_history, jnp.swapaxes(misfit, 0, 1))
    return jnp.swapaxes(solved_all, 0, 1)
```

```python
import jax
import jax.numpy as jnp
from jax import lax
from jax.experimental import pallas as pl
from jax.experimental.pallas import tpu as pltpu
from jax.sharding import PartitionSpec as P

REACH = 12
LANES = 128


def from_behind(block, axis, distance):
    devices = range(lax.axis_size(axis))
    route = [(i - distance, i) for i in devices if i - distance in devices]
    return lax.ppermute(block, axis, route)


def sent_to_all(array, axis):
    length = lax.axis_size(axis)
    return lax.all_to_all(
        jnp.broadcast_to(array[None], (length, *array.shape)), axis, 0, 0, tiled=True
    )


def row_chunks(rows):
    return [(start, min(LANES, rows - start)) for start in range(0, rows, LANES)]


def chain_kernel(lags, steps, sensors, factors_ref, forcing_ref, solved_ref, later_ref):
    ahead = lags - 1
    width = factors_ref.shape[2]
    pieces = range(width // LANES)
    later_ref[...] = jnp.zeros_like(later_ref)
    for row in range(ahead):
        solved_ref[row] = jnp.zeros((1, width), jnp.float32)

    def lanes(piece):
        return slice(piece * LANES, (piece + 1) * LANES)

    def step(t, unused):
        diagonal = lax.broadcasted_iota(jnp.int32, (LANES, LANES), 0) == lax.broadcasted_iota(
            jnp.int32, (LANES, LANES), 1
        )
        behind = [
            [
                jnp.broadcast_to(solved_ref[t + ahead - 1 - back, :, lanes(c)], (8, LANES))
                for c in pieces
            ]
            for back in range(ahead)
        ]
        for piece, (start, rows) in enumerate(row_chunks(sensors)):
            sums = []
            for row in range(start, start + rows, 8):
                total = later_ref[row : row + 8, :]
                for c in pieces:
                    total = total + factors_ref[0, row : row + 8, lanes(c)] * behind[0][c]
                sums.append(total)
            column = jnp.sum(jnp.concatenate(sums, axis=0), axis=1, keepdims=True)
            line = jnp.sum(jnp.where(diagonal[:rows], column, 0.0), axis=0, keepdims=True)
            solved_ref[t + ahead, :, lanes(piece)] = line + forcing_ref[t, :, lanes(piece)]
        for start in range(0, sensors, 8):
            total = None
            for back in range(ahead):
                for c in pieces:
                    term = factors_ref[back + 1, start : start + 8, lanes(c)] * behind[back][c]
                    total = term if total is None else total + term
            later_ref[start : start + 8, :] = total
        return unused

    lax.fori_loop(0, steps, step, 0)


def run_chain(factors, forcing):
    lags, sensors, width = factors.shape
    steps = forcing.shape[0]
    solved = pl.pallas_call(
        lambda *refs: chain_kernel(lags, steps, sensors, *refs),
        out_shape=jax.ShapeDtypeStruct((steps + lags - 1, 1, width), jnp.float32),
        in_specs=[pl.BlockSpec(memory_space=pltpu.VMEM)] * 2,
        out_specs=pl.BlockSpec(memory_space=pltpu.VMEM),
        scratch_shapes=[pltpu.VMEM((sensors, LANES), jnp.float32)],
        name="chain",
    )(factors, forcing.reshape(steps, 1, width))
    return solved[lags - 1 :, 0, :]


def per_device(params, kernel, lag_offsets, observed, diag_inverse, coupling):
    samples, step_count, col_count = params.shape
    lag_count, unused_cols, sensors = kernel.shape
    width = -(-sensors // LANES) * LANES
    exact = lax.Precision.HIGHEST
    flat_kernel = kernel.reshape(lag_count * col_count, sensors)
    rim = from_behind(params[:, step_count - (REACH - 1) :, :], "tm", 1)
    source = jnp.concatenate([rim, params], axis=1)
    windows = [
        lax.dynamic_slice_in_dim(source, REACH - 1 - lag_offsets[lag_index], step_count, 1)
        for lag_index in range(lag_count)
    ]
    stacked = jnp.stack(windows, axis=2).reshape(samples * step_count, lag_count * col_count)
    product = jnp.dot(stacked, flat_kernel, preferred_element_type=jnp.float32)
    local = product.reshape(samples, step_count, sensors)
    group = lax.axis_size("param")
    share = samples // group
    parts = lax.all_to_all(
        local.reshape(group, share, step_count, sensors), "param", 0, 0, tiled=True
    )
    summed = jnp.sum(parts, axis=0)
    mine = lax.dynamic_slice_in_dim(observed, lax.axis_index("param") * share, share, 0)
    misfit = mine.astype(jnp.float32) - summed

    factors = -jnp.einsum("mi,jin->jmn", diag_inverse, coupling, precision=exact)
    factors = jnp.pad(factors, ((0, 0), (0, 0), (0, width - sensors)))
    forcing = jnp.einsum("stn,mn->stm", misfit, diag_inverse, precision=exact)
    forcing = jnp.pad(forcing, ((0, 0), (0, 0), (0, width - sensors)))
    every = sent_to_all(forcing, "tm")
    every = jnp.moveaxis(every, 0, 1).reshape(share, -1, width)
    solved = jnp.stack([run_chain(factors, every[s]) for s in range(share)])
    own = lax.dynamic_slice_in_dim(solved, lax.axis_index("tm") * step_count, step_count, 1)
    own = own[:, :, :sensors]
    parts = sent_to_all(own, "param")
    return parts.reshape(samples, step_count, sensors)


def solution(mesh):
    in_specs = (P(None, "tm", "param"), P(None, "param", None), P(), P(None, "tm", None), P(), P())
    out_specs = P(None, "tm", None)
    return jax.shard_map(
        per_device, mesh=mesh, in_specs=in_specs, out_specs=out_specs, check_vma=False
    )
```

```python
import functools

import jax
import jax.numpy as jnp
from jax import lax
from jax.experimental import pallas as pl
from jax.experimental.pallas import tpu as pltpu
from jax.sharding import PartitionSpec as P

REACH = 12
LANES = 128
LEVELS = 32700.0
OCTAVE = 64.0
TINY = 1e-37


def from_behind(block, axis, distance):
    devices = range(lax.axis_size(axis))
    route = [(i - distance, i) for i in devices if i - distance in devices]
    return lax.ppermute(block, axis, route)


def sent_to_all(array, axis):
    length = lax.axis_size(axis)
    return lax.all_to_all(
        jnp.broadcast_to(array[None], (length, *array.shape)), axis, 0, 0, tiled=True
    )


def grade_of(rows):
    largest = jnp.maximum(jnp.max(jnp.abs(rows), axis=-1, keepdims=True), TINY)
    return jnp.ceil(jnp.log2(largest) * OCTAVE)


def coded(rows, grade):
    return jnp.round(rows * (LEVELS * jnp.exp2(grade * (-1.0 / OCTAVE))))


def scale_of(grade):
    return jnp.exp2(grade * (1.0 / OCTAVE)) * (1.0 / LEVELS)


def row_chunks(rows):
    return [(start, min(LANES, rows - start)) for start in range(0, rows, LANES)]


def chain_kernel(
    block, sensors, near_ref, two_hi, two_lo, three_hi, three_lo, forcing_ref,
    code_ref, solved_ref, later_ref, carry_ref, even_ref, odd_ref, far_ref,
):
    width = near_ref.shape[2]
    pieces = list(range(width // LANES))
    reach = two_hi.shape[0]
    rest = [c for c in pieces if c * LANES >= reach]
    for ref in (later_ref, carry_ref, even_ref, odd_ref):
        ref[...] = jnp.zeros_like(ref)
    dot = functools.partial(jnp.dot, preferred_element_type=jnp.float32)

    def lanes(piece):
        return slice(piece * LANES, (piece + 1) * LANES)

    def wide(row):
        return jnp.broadcast_to(row, (8, LANES))

    def pair(turn, unused):
        diagonal = lax.broadcasted_iota(jnp.int32, (LANES, LANES), 0) == lax.broadcasted_iota(
            jnp.int32, (LANES, LANES), 1
        )
        row_id = lax.broadcasted_iota(jnp.int32, (16, LANES), 0)
        split = []
        for c in pieces:
            older = jnp.concatenate([even_ref[:, lanes(c)]] * 2, axis=0)
            newer = jnp.concatenate([odd_ref[:, lanes(c)]] * 2, axis=0)
            both = jnp.where(row_id < 2, older, jnp.where(row_id < 4, newer, 0.0))
            high = both.astype(jnp.bfloat16).astype(jnp.float32)
            split.append(
                jnp.where((row_id == 0) | (row_id == 2), high, both - high).astype(jnp.bfloat16)
            )
        operand = jnp.concatenate(split, axis=1)
        front = operand[:, :reach]
        far_ref[0] = dot(front, two_hi[...]) + dot(front, two_lo[...])
        far_ref[1] = dot(operand, three_hi[...]) + dot(operand, three_lo[...])

        for half in range(2):
            t = 2 * turn + half
            prev_ref, new_ref = ((odd_ref, even_ref), (even_ref, odd_ref))[half]
            behind = [prev_ref[:, lanes(c)] for c in pieces]
            for piece, (start, rows) in enumerate(row_chunks(sensors)):
                sums = []
                for row in range(start, start + rows, 8):
                    total = later_ref[row : row + 8, :]
                    for c in pieces:
                        total = total + near_ref[0, row : row + 8, lanes(c)] * behind[c]
                    sums.append(total)
                column = jnp.sum(jnp.concatenate(sums, axis=0), axis=1, keepdims=True)
                line = jnp.sum(jnp.where(diagonal[:rows], column, 0.0), axis=0, keepdims=True)
                base = wide(forcing_ref[t, :, lanes(piece)])
                if half == 0:
                    base = base + wide(carry_ref[0:1, lanes(piece)])
                else:
                    base = base + (
                        wide(far_ref[1, 0:1, lanes(piece)]) + wide(far_ref[1, 1:2, lanes(piece)])
                    )
                base = base + (
                    wide(far_ref[0, 2 * half : 2 * half + 1, lanes(piece)])
                    + wide(far_ref[0, 2 * half + 1 : 2 * half + 2, lanes(piece)])
                )
                solved = wide(line) + base
                new_ref[:, lanes(piece)] = solved
                solved_ref[lax.rem(t, block), :, lanes(piece)] = solved[0:1]
            behind = {c: prev_ref[:, lanes(c)] for c in rest}
            for start in range(0, sensors, 8):
                total = None
                for c in rest:
                    term = near_ref[1, start : start + 8, lanes(c)] * behind[c]
                    total = term if total is None else total + term
                later_ref[start : start + 8, :] = total
        carry_ref[0:1, :] = far_ref[1, 2:3] + far_ref[1, 3:4]
        return unused

    turns = (lax.axis_index("tm") + 1) * (block // 2)
    lax.fori_loop(0, turns, pair, 0)
    own = jnp.concatenate([solved_ref[row] for row in range(block)], axis=0)
    grade = grade_of(own)
    place = lax.broadcasted_iota(jnp.int32, own.shape, 1)
    code = jnp.where(place == sensors, grade, coded(own, grade))
    code_ref[...] = code.astype(jnp.int32).astype(jnp.int16)


def run_chain(block, near, two_hi, two_lo, three_hi, three_lo, forcing):
    unused_lags, sensors, width = near.shape
    steps = forcing.shape[0]
    code, unused_rows = pl.pallas_call(
        functools.partial(chain_kernel, block, sensors),
        out_shape=(
            jax.ShapeDtypeStruct((block, width), jnp.int16),
            jax.ShapeDtypeStruct((block, 1, width), jnp.float32),
        ),
        in_specs=[pl.BlockSpec(memory_space=pltpu.VMEM)] * 6,
        out_specs=[pl.BlockSpec(memory_space=pltpu.VMEM)] * 2,
        scratch_shapes=[
            pltpu.VMEM((sensors, LANES), jnp.float32),
            pltpu.VMEM((8, width), jnp.float32),
            pltpu.VMEM((8, width), jnp.float32),
            pltpu.VMEM((8, width), jnp.float32),
            pltpu.VMEM((2, 16, width), jnp.float32),
        ],
        name="chain",
    )(near, two_hi, two_lo, three_hi, three_lo, forcing.reshape(steps, 1, width))
    return code


def high_low(array):
    high = array.astype(jnp.bfloat16).astype(jnp.float32)
    return high.astype(jnp.bfloat16), (array - high).astype(jnp.bfloat16)


def factor(diag_ref, coupling_ref, lag):
    sensors = diag_ref.shape[0]
    lines = []
    for start in range(0, sensors, 2 * LANES):
        end = min(start + 2 * LANES, sensors)
        lines.append(
            -jnp.dot(
                diag_ref[start:end, :end],
                coupling_ref[lag, :end, :],
                precision=lax.Precision.HIGHEST,
                preferred_element_type=jnp.float32,
            )
        )
    return jnp.concatenate(lines, axis=0)


def turned(square_ref, high_ref, low_ref):
    for row in range(0, high_ref.shape[0], LANES):
        for column in range(0, high_ref.shape[1], LANES):
            tile = square_ref[column : column + LANES, row : row + LANES].T
            high, low = high_low(tile)
            high_ref[row : row + LANES, column : column + LANES] = high
            low_ref[row : row + LANES, column : column + LANES] = low


def near_kernel(diag_ref, coupling_ref, near_ref, high_ref, low_ref, square_ref):
    sensors = diag_ref.shape[0]
    near_ref[...] = jnp.zeros_like(near_ref)
    square_ref[...] = jnp.zeros_like(square_ref)
    near_ref[0, :, :sensors] = factor(diag_ref, coupling_ref, 0)
    second = factor(diag_ref, coupling_ref, 1)
    near_ref[1, :, :sensors] = second
    square_ref[:sensors, :sensors] = second
    turned(square_ref, high_ref, low_ref)


def far_kernel(diag_ref, coupling_ref, high_ref, low_ref, square_ref):
    sensors = diag_ref.shape[0]
    square_ref[...] = jnp.zeros_like(square_ref)
    square_ref[:sensors, :sensors] = factor(diag_ref, coupling_ref, 0)
    turned(square_ref, high_ref, low_ref)


def prepare_near(diag_inverse, coupling, width):
    sensors = diag_inverse.shape[0]
    part = jax.ShapeDtypeStruct((2 * LANES, width), jnp.bfloat16)
    return pl.pallas_call(
        near_kernel,
        out_shape=(jax.ShapeDtypeStruct((2, sensors, width), jnp.float32), part, part),
        in_specs=[
            pl.BlockSpec((sensors, sensors), lambda _: (0, 0)),
            pl.BlockSpec((2, sensors, sensors), lambda _: (0, 0, 0)),
        ],
        out_specs=[
            pl.BlockSpec((2, sensors, width), lambda _: (0, 0, 0)),
            pl.BlockSpec((2 * LANES, width), lambda _: (0, 0)),
            pl.BlockSpec((2 * LANES, width), lambda _: (0, 0)),
        ],
        grid=(1,),
        scratch_shapes=[pltpu.VMEM((width, width), jnp.float32)],
        cost_estimate=pl.CostEstimate(
            flops=12 * 2 * sensors**3, bytes_accessed=16 * sensors**2, transcendentals=0
        ),
        name="near_factors",
    )(diag_inverse, coupling)


def prepare_far(diag_inverse, coupling, width):
    sensors = diag_inverse.shape[0]
    part = jax.ShapeDtypeStruct((width, width), jnp.bfloat16)
    return pl.pallas_call(
        far_kernel,
        out_shape=(part, part),
        in_specs=[
            pl.BlockSpec((sensors, sensors), lambda _: (0, 0)),
            pl.BlockSpec((1, sensors, sensors), lambda _: (2, 0, 0)),
        ],
        out_specs=[pl.BlockSpec((width, width), lambda _: (0, 0))] * 2,
        grid=(1,),
        scratch_shapes=[pltpu.VMEM((width, width), jnp.float32)],
        cost_estimate=pl.CostEstimate(
            flops=12 * sensors**3, bytes_accessed=12 * sensors**2, transcendentals=0
        ),
        name="far_factors",
    )(diag_inverse, coupling)


def predict_kernel(offsets_ref, source_ref, kernel_ref, code_ref, total_ref):
    steps, samples, cols = code_ref.shape[0], source_ref.shape[1], source_ref.shape[2]
    sensors = kernel_ref.shape[2]
    lag = pl.program_id(0)
    window = source_ref[pl.ds(REACH - 1 - offsets_ref[lag], steps)]
    product = jnp.dot(
        window.reshape(steps * samples, cols), kernel_ref[0], preferred_element_type=jnp.float32
    )

    @pl.when(lag == 0)
    def first():
        total_ref[...] = product

    @pl.when(lag > 0)
    def later():
        total_ref[...] = total_ref[...] + product

    @pl.when(lag == pl.num_programs(0) - 1)
    def last():
        for step in range(steps):
            rows = total_ref[step * samples : (step + 1) * samples, :]
            grade = grade_of(rows)
            code = coded(rows, grade)
            code_ref[step, :, :sensors] = code.astype(jnp.int32).astype(jnp.int16)
            code_ref[step, :, sensors : sensors + 1] = grade.astype(jnp.int32).astype(jnp.int16)


def predict(source, kernel, lag_offsets):
    lag_count, cols, sensors = kernel.shape
    span, samples, unused_cols = source.shape
    steps = span - (REACH - 1)
    return pl.pallas_call(
        predict_kernel,
        out_shape=jax.ShapeDtypeStruct((steps, samples, sensors + 1), jnp.int16),
        in_specs=[
            pl.BlockSpec(memory_space=pltpu.SMEM),
            pl.BlockSpec((span, samples, cols), lambda lag: (0, 0, 0)),
            pl.BlockSpec((1, cols, sensors), lambda lag: (lag, 0, 0)),
        ],
        out_specs=pl.BlockSpec((steps, samples, sensors + 1), lambda lag: (0, 0, 0)),
        grid=(lag_count,),
        scratch_shapes=[pltpu.VMEM((steps * samples, sensors), jnp.float32)],
        cost_estimate=pl.CostEstimate(
            flops=2 * steps * samples * lag_count * cols * sensors,
            bytes_accessed=2 * lag_count * cols * sensors,
            transcendentals=0,
        ),
        name="predict",
    )(lag_offsets, source, kernel)


def per_device(params, kernel, lag_offsets, observed, diag_inverse, coupling):
    samples, step_count, col_count = params.shape
    lag_count, unused_cols, sensors = kernel.shape
    width = -(-sensors // LANES) * LANES
    exact = lax.Precision.HIGHEST
    group = lax.axis_size("param")
    share = samples // group
    by_step = jnp.swapaxes(params, 0, 1)
    rim = from_behind(by_step[step_count - (REACH - 1) :], "tm", 1)
    near = prepare_near(diag_inverse, coupling, width)
    rim, near = lax.optimization_barrier((rim, near))
    code = predict(jnp.concatenate([rim, by_step], axis=0), kernel, lag_offsets)
    code = jnp.swapaxes(code, 0, 1).reshape(group, share, step_count, sensors + 1)
    code = lax.all_to_all(code, "param", 0, 0, tiled=True)
    far = prepare_far(diag_inverse, coupling, width)
    code, far = lax.optimization_barrier((code, far))
    factors = (*near, *far)
    grade = code[..., sensors:].astype(jnp.float32)
    summed = jnp.sum(code[..., :sensors].astype(jnp.float32) * scale_of(grade), axis=0)
    mine = lax.dynamic_slice_in_dim(observed, lax.axis_index("param") * share, share, 0)
    misfit = mine.astype(jnp.float32) - summed

    forcing = jnp.einsum("stn,mn->stm", misfit, diag_inverse, precision=exact)
    forcing = jnp.pad(forcing, ((0, 0), (0, 0), (0, width - sensors)))
    every = sent_to_all(forcing, "tm")
    every = jnp.moveaxis(every, 0, 1).reshape(share, -1, width)
    code = jnp.stack([run_chain(step_count, *factors, every[s]) for s in range(share)])
    code = sent_to_all(code, "param").reshape(samples, step_count, width)
    grade = code[..., sensors : sensors + 1].astype(jnp.float32)
    return code[..., :sensors].astype(jnp.float32) * scale_of(grade)


def solution(mesh):
    in_specs = (P(None, "tm", "param"), P(None, "param", None), P(), P(None, "tm", None), P(), P())
    out_specs = P(None, "tm", None)
    return jax.shard_map(
        per_device, mesh=mesh, in_specs=in_specs, out_specs=out_specs, check_vma=False
    )
```

```python
import functools

import jax
import jax.numpy as jnp
from jax import lax
from jax.experimental import pallas as pl
from jax.experimental.pallas import tpu as pltpu
from jax.sharding import PartitionSpec as P

REACH = 12
LANES = 128
LEVELS = 32700.0
OCTAVE = 64.0
TINY = 1e-37


def from_behind(block, axis, distance):
    devices = range(lax.axis_size(axis))
    route = [(i - distance, i) for i in devices if i - distance in devices]
    return lax.ppermute(block, axis, route)


def sent_to_all(array, axis):
    length = lax.axis_size(axis)
    return lax.all_to_all(
        jnp.broadcast_to(array[None], (length, *array.shape)), axis, 0, 0, tiled=True
    )


def grade_of(rows):
    largest = jnp.maximum(jnp.max(jnp.abs(rows), axis=-1, keepdims=True), TINY)
    return jnp.ceil(jnp.log2(largest) * OCTAVE)


def coded(rows, grade):
    return jnp.round(rows * (LEVELS * jnp.exp2(grade * (-1.0 / OCTAVE))))


def scale_of(grade):
    return jnp.exp2(grade * (1.0 / OCTAVE)) * (1.0 / LEVELS)


def row_chunks(rows):
    return [(start, min(LANES, rows - start)) for start in range(0, rows, LANES)]


def chain_kernel(
    block, sensors, near_ref, two_hi, two_lo, three_hi, three_lo, forcing_ref,
    code_ref, solved_ref, later_ref, carry_ref, even_ref, odd_ref, far_ref,
):
    width = near_ref.shape[2]
    pieces = list(range(width // LANES))
    reach = two_hi.shape[0]
    rest = [c for c in pieces if c * LANES >= reach]
    for ref in (later_ref, carry_ref, even_ref, odd_ref):
        ref[...] = jnp.zeros_like(ref)
    dot = functools.partial(jnp.dot, preferred_element_type=jnp.float32)

    def lanes(piece):
        return slice(piece * LANES, (piece + 1) * LANES)

    def wide(row):
        return jnp.broadcast_to(row, (8, LANES))

    def pair(turn, unused):
        diagonal = lax.broadcasted_iota(jnp.int32, (LANES, LANES), 0) == lax.broadcasted_iota(
            jnp.int32, (LANES, LANES), 1
        )
        row_id = lax.broadcasted_iota(jnp.int32, (16, LANES), 0)
        split = []
        for c in pieces:
            older = jnp.concatenate([even_ref[:, lanes(c)]] * 2, axis=0)
            newer = jnp.concatenate([odd_ref[:, lanes(c)]] * 2, axis=0)
            both = jnp.where(row_id < 2, older, jnp.where(row_id < 4, newer, 0.0))
            high = both.astype(jnp.bfloat16).astype(jnp.float32)
            split.append(
                jnp.where((row_id == 0) | (row_id == 2), high, both - high).astype(jnp.bfloat16)
            )
        operand = jnp.concatenate(split, axis=1)
        front = operand[:, :reach]
        far_ref[0] = dot(front, two_hi[...]) + dot(front, two_lo[...])
        far_ref[1] = dot(operand, three_hi[...]) + dot(operand, three_lo[...])

        for half in range(2):
            t = 2 * turn + half
            prev_ref, new_ref = ((odd_ref, even_ref), (even_ref, odd_ref))[half]
            behind = [prev_ref[:, lanes(c)] for c in pieces]
            for piece, (start, rows) in enumerate(row_chunks(sensors)):
                sums = []
                for row in range(start, start + rows, 8):
                    total = later_ref[row : row + 8, :]
                    for c in pieces:
                        total = total + near_ref[0, row : row + 8, lanes(c)] * behind[c]
                    sums.append(total)
                column = jnp.sum(jnp.concatenate(sums, axis=0), axis=1, keepdims=True)
                line = jnp.sum(jnp.where(diagonal[:rows], column, 0.0), axis=0, keepdims=True)
                base = wide(forcing_ref[t, :, lanes(piece)])
                if half == 0:
                    base = base + wide(carry_ref[0:1, lanes(piece)])
                else:
                    base = base + (
                        wide(far_ref[1, 0:1, lanes(piece)]) + wide(far_ref[1, 1:2, lanes(piece)])
                    )
                base = base + (
                    wide(far_ref[0, 2 * half : 2 * half + 1, lanes(piece)])
                    + wide(far_ref[0, 2 * half + 1 : 2 * half + 2, lanes(piece)])
                )
                solved = wide(line) + base
                new_ref[:, lanes(piece)] = solved
                solved_ref[lax.rem(t, block), :, lanes(piece)] = solved[0:1]
            gate = jnp.minimum(jnp.abs(sums[-1]), 0.0)
            behind = {c: prev_ref[:, lanes(c)] + gate for c in rest}
            for start in range(0, sensors, 8):
                total = None
                for c in rest:
                    term = near_ref[1, start : start + 8, lanes(c)] * behind[c]
                    total = term if total is None else total + term
                later_ref[start : start + 8, :] = total
        carry_ref[0:1, :] = far_ref[1, 2:3] + far_ref[1, 3:4]
        return unused

    turns = (lax.axis_index("tm") + 1) * (block // 2)
    def several(group, unused):
        for member in range(4):
            unused = pair(4 * group + member, unused)
        return unused

    lax.fori_loop(0, turns // 4, several, 0)
    own = jnp.concatenate([solved_ref[row] for row in range(block)], axis=0)
    grade = grade_of(own)
    place = lax.broadcasted_iota(jnp.int32, own.shape, 1)
    code = jnp.where(place == sensors, grade, coded(own, grade))
    code_ref[...] = code.astype(jnp.int32).astype(jnp.int16)


def run_chain(block, near, two_hi, two_lo, three_hi, three_lo, forcing):
    unused_lags, sensors, width = near.shape
    steps = forcing.shape[0]
    code, unused_rows = pl.pallas_call(
        functools.partial(chain_kernel, block, sensors),
        out_shape=(
            jax.ShapeDtypeStruct((block, width), jnp.int16),
            jax.ShapeDtypeStruct((block, 1, width), jnp.float32),
        ),
        in_specs=[pl.BlockSpec(memory_space=pltpu.VMEM)] * 6,
        out_specs=[pl.BlockSpec(memory_space=pltpu.VMEM)] * 2,
        scratch_shapes=[
            pltpu.VMEM((sensors, LANES), jnp.float32),
            pltpu.VMEM((8, width), jnp.float32),
            pltpu.VMEM((8, width), jnp.float32),
            pltpu.VMEM((8, width), jnp.float32),
            pltpu.VMEM((2, 16, width), jnp.float32),
        ],
        name="chain",
    )(near, two_hi, two_lo, three_hi, three_lo, forcing.reshape(steps, 1, width))
    return code


def high_low(array):
    high = array.astype(jnp.bfloat16).astype(jnp.float32)
    return high.astype(jnp.bfloat16), (array - high).astype(jnp.bfloat16)


def factor(diag_ref, coupling_ref, lag):
    sensors = diag_ref.shape[0]
    lines = []
    for start in range(0, sensors, 2 * LANES):
        end = min(start + 2 * LANES, sensors)
        lines.append(
            -jnp.dot(
                diag_ref[start:end, :end],
                coupling_ref[lag, :end, :],
                precision=lax.Precision.HIGHEST,
                preferred_element_type=jnp.float32,
            )
        )
    return jnp.concatenate(lines, axis=0)


def turned(square_ref, high_ref, low_ref):
    for row in range(0, high_ref.shape[0], LANES):
        for column in range(0, high_ref.shape[1], LANES):
            tile = square_ref[column : column + LANES, row : row + LANES].T
            high, low = high_low(tile)
            high_ref[row : row + LANES, column : column + LANES] = high
            low_ref[row : row + LANES, column : column + LANES] = low


def near_kernel(diag_ref, coupling_ref, near_ref, high_ref, low_ref, square_ref):
    sensors = diag_ref.shape[0]
    near_ref[...] = jnp.zeros_like(near_ref)
    square_ref[...] = jnp.zeros_like(square_ref)
    near_ref[0, :, :sensors] = factor(diag_ref, coupling_ref, 0)
    second = factor(diag_ref, coupling_ref, 1)
    near_ref[1, :, :sensors] = second
    square_ref[:sensors, :sensors] = second
    turned(square_ref, high_ref, low_ref)


def far_kernel(diag_ref, coupling_ref, high_ref, low_ref, square_ref):
    sensors = diag_ref.shape[0]
    square_ref[...] = jnp.zeros_like(square_ref)
    square_ref[:sensors, :sensors] = factor(diag_ref, coupling_ref, 0)
    turned(square_ref, high_ref, low_ref)


def prepare_near(diag_inverse, coupling, width):
    sensors = diag_inverse.shape[0]
    part = jax.ShapeDtypeStruct((2 * LANES, width), jnp.bfloat16)
    return pl.pallas_call(
        near_kernel,
        out_shape=(jax.ShapeDtypeStruct((2, sensors, width), jnp.float32), part, part),
        in_specs=[
            pl.BlockSpec((sensors, sensors), lambda _: (0, 0)),
            pl.BlockSpec((2, sensors, sensors), lambda _: (0, 0, 0)),
        ],
        out_specs=[
            pl.BlockSpec((2, sensors, width), lambda _: (0, 0, 0)),
            pl.BlockSpec((2 * LANES, width), lambda _: (0, 0)),
            pl.BlockSpec((2 * LANES, width), lambda _: (0, 0)),
        ],
        grid=(1,),
        scratch_shapes=[pltpu.VMEM((width, width), jnp.float32)],
        cost_estimate=pl.CostEstimate(
            flops=12 * 2 * sensors**3, bytes_accessed=16 * sensors**2, transcendentals=0
        ),
        name="near_factors",
    )(diag_inverse, coupling)


def prepare_far(diag_inverse, coupling, width):
    sensors = diag_inverse.shape[0]
    part = jax.ShapeDtypeStruct((width, width), jnp.bfloat16)
    return pl.pallas_call(
        far_kernel,
        out_shape=(part, part),
        in_specs=[
            pl.BlockSpec((sensors, sensors), lambda _: (0, 0)),
            pl.BlockSpec((1, sensors, sensors), lambda _: (2, 0, 0)),
        ],
        out_specs=[pl.BlockSpec((width, width), lambda _: (0, 0))] * 2,
        grid=(1,),
        scratch_shapes=[pltpu.VMEM((width, width), jnp.float32)],
        cost_estimate=pl.CostEstimate(
            flops=12 * sensors**3, bytes_accessed=12 * sensors**2, transcendentals=0
        ),
        name="far_factors",
    )(diag_inverse, coupling)


def predict_kernel(offsets_ref, source_ref, kernel_ref, code_ref, total_ref):
    steps, samples, cols = code_ref.shape[0], source_ref.shape[1], source_ref.shape[2]
    sensors = kernel_ref.shape[1]
    lag = pl.program_id(0)
    window = source_ref[pl.ds(REACH - 1 - offsets_ref[lag], steps)]
    product = lax.dot_general(
        window.reshape(steps * samples, cols),
        kernel_ref[0],
        (((1,), (1,)), ((), ())),
        preferred_element_type=jnp.float32,
    )

    @pl.when(lag == 0)
    def first():
        total_ref[...] = product

    @pl.when(lag > 0)
    def later():
        total_ref[...] = total_ref[...] + product

    @pl.when(lag == pl.num_programs(0) - 1)
    def last():
        for step in range(steps):
            rows = total_ref[step * samples : (step + 1) * samples, :]
            grade = grade_of(rows)
            code = coded(rows, grade)
            code_ref[step, :, :sensors] = code.astype(jnp.int32).astype(jnp.int16)
            code_ref[step, :, sensors : sensors + 1] = grade.astype(jnp.int32).astype(jnp.int16)


def predict(source, kernel, lag_offsets):
    lag_count, sensors, cols = kernel.shape
    span, samples, unused_cols = source.shape
    steps = span - (REACH - 1)
    return pl.pallas_call(
        predict_kernel,
        out_shape=jax.ShapeDtypeStruct((steps, samples, sensors + 1), jnp.int16),
        in_specs=[
            pl.BlockSpec(memory_space=pltpu.SMEM),
            pl.BlockSpec((span, samples, cols), lambda lag: (0, 0, 0)),
            pl.BlockSpec((1, sensors, cols), lambda lag: (lag, 0, 0)),
        ],
        out_specs=pl.BlockSpec((steps, samples, sensors + 1), lambda lag: (0, 0, 0)),
        grid=(lag_count,),
        scratch_shapes=[pltpu.VMEM((steps * samples, sensors), jnp.float32)],
        cost_estimate=pl.CostEstimate(
            flops=2 * steps * samples * lag_count * cols * sensors,
            bytes_accessed=2 * lag_count * cols * sensors,
            transcendentals=0,
        ),
        name="predict",
    )(lag_offsets, source, kernel)


def forcing_kernel(code_ref, observed_ref, diag_ref, forcing_ref):
    sensors = diag_ref.shape[0]
    total = None
    for part in range(code_ref.shape[0]):
        code = code_ref[part].astype(jnp.int32).astype(jnp.float32)
        term = code * scale_of(code[:, sensors : sensors + 1])
        total = term if total is None else total + term
    misfit = observed_ref[...] - total[:, :sensors]
    rows = lax.dot_general(
        misfit,
        diag_ref[...],
        (((1,), (1,)), ((), ())),
        precision=lax.Precision.HIGHEST,
        preferred_element_type=jnp.float32,
    )
    for copy in range(forcing_ref.shape[0]):
        forcing_ref[copy] = jnp.zeros(forcing_ref.shape[1:], jnp.float32)
        forcing_ref[copy, :, :sensors] = rows


def force(code, observed, diag_inverse, copies, width):
    steps = code.shape[1]
    return pl.pallas_call(
        forcing_kernel,
        out_shape=jax.ShapeDtypeStruct((copies, steps, width), jnp.float32),
        in_specs=[pl.BlockSpec(memory_space=pltpu.VMEM)] * 3,
        out_specs=pl.BlockSpec(memory_space=pltpu.VMEM),
        name="forcing",
    )(code, observed, diag_inverse)


def per_device(params, kernel, lag_offsets, observed, diag_inverse, coupling):
    samples, step_count, col_count = params.shape
    lag_count, unused_cols, sensors = kernel.shape
    width = -(-sensors // LANES) * LANES
    group = lax.axis_size("param")
    share = samples // group
    by_step = jnp.swapaxes(params, 0, 1)
    rim = from_behind(by_step[step_count - (REACH - 1) :], "tm", 1)
    near = prepare_near(diag_inverse, coupling, width)
    rim, near = lax.optimization_barrier((rim, near))
    code = predict(
        jnp.concatenate([rim, by_step], axis=0), jnp.swapaxes(kernel, 1, 2), lag_offsets
    )
    code = jnp.swapaxes(code, 0, 1).reshape(group, share, step_count, sensors + 1)
    code = lax.all_to_all(code, "param", 0, 0, tiled=True)
    far = prepare_far(diag_inverse, coupling, width)
    code, far = lax.optimization_barrier((code, far))
    factors = (*near, *far)
    mine = lax.dynamic_slice_in_dim(observed, lax.axis_index("param") * share, share, 0)
    mine = mine.astype(jnp.float32)
    blocks = lax.axis_size("tm")
    every = [force(code[:, s], mine[s], diag_inverse, blocks, width) for s in range(share)]
    every = lax.all_to_all(jnp.stack(every, axis=1), "tm", 0, 0, tiled=True)
    every = jnp.moveaxis(every, 0, 1).reshape(share, -1, width)
    code = jnp.stack([run_chain(step_count, *factors, every[s]) for s in range(share)])
    code = sent_to_all(code, "param").reshape(samples, step_count, width)
    grade = code[..., sensors : sensors + 1].astype(jnp.float32)
    return code[..., :sensors].astype(jnp.float32) * scale_of(grade)


def solution(mesh):
    in_specs = (P(None, "tm", "param"), P(None, "param", None), P(), P(None, "tm", None), P(), P())
    out_specs = P(None, "tm", None)
    return jax.shard_map(
        per_device, mesh=mesh, in_specs=in_specs, out_specs=out_specs, check_vma=False
    )
```

```python
import functools

import jax
import jax.numpy as jnp
from jax import lax
from jax.experimental import pallas as pl
from jax.experimental.pallas import tpu as pltpu
from jax.sharding import PartitionSpec as P

REACH = 12
LANES = 128
LEVELS = 32700.0
OCTAVE = 64.0
TINY = 1e-37


def from_behind(block, axis, distance):
    devices = range(lax.axis_size(axis))
    route = [(i - distance, i) for i in devices if i - distance in devices]
    return lax.ppermute(block, axis, route)


def grade_of(rows):
    largest = jnp.maximum(jnp.max(jnp.abs(rows), axis=-1, keepdims=True), TINY)
    return jnp.ceil(jnp.log2(largest) * OCTAVE)


def coded(rows, grade):
    return jnp.round(rows * (LEVELS * jnp.exp2(grade * (-1.0 / OCTAVE))))


def scale_of(grade):
    return jnp.exp2(grade * (1.0 / OCTAVE)) * (1.0 / LEVELS)


def coded_with_grade(rows, place):
    grade = grade_of(rows)
    lane = lax.broadcasted_iota(jnp.int32, rows.shape, 1)
    code = jnp.where(lane == place, grade, coded(rows, grade))
    return code.astype(jnp.int32).astype(jnp.int16)


def row_chunks(rows):
    return [(start, min(LANES, rows - start)) for start in range(0, rows, LANES)]


def chain_kernel(
    block, sensors, near_ref, two_hi, two_lo, three_hi, three_lo, forcing_ref,
    code_ref, solved_ref, later_ref, carry_ref, even_ref, odd_ref, far_ref,
):
    width = near_ref.shape[2]
    pieces = list(range(width // LANES))
    reach = two_hi.shape[0]
    rest = [c for c in pieces if c * LANES >= reach]
    for ref in (later_ref, carry_ref, even_ref, odd_ref):
        ref[...] = jnp.zeros_like(ref)
    dot = functools.partial(jnp.dot, preferred_element_type=jnp.float32)

    def lanes(piece):
        return slice(piece * LANES, (piece + 1) * LANES)

    def wide(row):
        return jnp.broadcast_to(row, (8, LANES))

    def pair(turn, unused):
        diagonal = lax.broadcasted_iota(jnp.int32, (LANES, LANES), 0) == lax.broadcasted_iota(
            jnp.int32, (LANES, LANES), 1
        )
        row_id = lax.broadcasted_iota(jnp.int32, (16, LANES), 0)
        split = []
        for c in pieces:
            older = jnp.concatenate([even_ref[:, lanes(c)]] * 2, axis=0)
            newer = jnp.concatenate([odd_ref[:, lanes(c)]] * 2, axis=0)
            both = jnp.where(row_id < 2, older, jnp.where(row_id < 4, newer, 0.0))
            high = both.astype(jnp.bfloat16).astype(jnp.float32)
            split.append(
                jnp.where((row_id == 0) | (row_id == 2), high, both - high).astype(jnp.bfloat16)
            )
        operand = jnp.concatenate(split, axis=1)
        front = operand[:, :reach]
        far_ref[0] = dot(front, two_hi[...]) + dot(front, two_lo[...])
        far_ref[1] = dot(operand, three_hi[...]) + dot(operand, three_lo[...])

        for half in range(2):
            t = 2 * turn + half
            prev_ref, new_ref = ((odd_ref, even_ref), (even_ref, odd_ref))[half]
            behind = [prev_ref[:, lanes(c)] for c in pieces]
            for piece, (start, rows) in enumerate(row_chunks(sensors)):
                sums = []
                for row in range(start, start + rows, 8):
                    total = later_ref[row : row + 8, :]
                    for c in pieces:
                        total = total + near_ref[0, row : row + 8, lanes(c)] * behind[c]
                    sums.append(total)
                column = jnp.sum(jnp.concatenate(sums, axis=0), axis=1, keepdims=True)
                line = jnp.sum(jnp.where(diagonal[:rows], column, 0.0), axis=0, keepdims=True)
                base = wide(forcing_ref[t, :, lanes(piece)])
                if half == 0:
                    base = base + wide(carry_ref[0:1, lanes(piece)])
                else:
                    base = base + (
                        wide(far_ref[1, 0:1, lanes(piece)]) + wide(far_ref[1, 1:2, lanes(piece)])
                    )
                base = base + (
                    wide(far_ref[0, 2 * half : 2 * half + 1, lanes(piece)])
                    + wide(far_ref[0, 2 * half + 1 : 2 * half + 2, lanes(piece)])
                )
                solved = wide(line) + base
                new_ref[:, lanes(piece)] = solved
                solved_ref[lax.rem(t, block), :, lanes(piece)] = solved[0:1]
            gate = jnp.minimum(jnp.abs(sums[-1]), 0.0)
            behind = {c: prev_ref[:, lanes(c)] + gate for c in rest}
            for start in range(0, sensors, 8):
                total = None
                for c in rest:
                    term = near_ref[1, start : start + 8, lanes(c)] * behind[c]
                    total = term if total is None else total + term
                later_ref[start : start + 8, :] = total
        carry_ref[0:1, :] = far_ref[1, 2:3] + far_ref[1, 3:4]
        return unused

    turns = (lax.axis_index("tm") + 1) * (block // 2)
    def several(group, unused):
        for member in range(4):
            unused = pair(4 * group + member, unused)
        return unused

    lax.fori_loop(0, turns // 4, several, 0)
    own = jnp.concatenate([solved_ref[row] for row in range(block)], axis=0)
    code = coded_with_grade(own, sensors)
    for copy in range(code_ref.shape[0]):
        code_ref[copy] = code


def run_chain(block, copies, near, two_hi, two_lo, three_hi, three_lo, forcing):
    unused_lags, sensors, width = near.shape
    steps = forcing.shape[0]
    code, unused_rows = pl.pallas_call(
        functools.partial(chain_kernel, block, sensors),
        out_shape=(
            jax.ShapeDtypeStruct((copies, block, width), jnp.int16),
            jax.ShapeDtypeStruct((block, 1, width), jnp.float32),
        ),
        in_specs=[pl.BlockSpec(memory_space=pltpu.VMEM)] * 6,
        out_specs=[pl.BlockSpec(memory_space=pltpu.VMEM)] * 2,
        scratch_shapes=[
            pltpu.VMEM((sensors, LANES), jnp.float32),
            pltpu.VMEM((8, width), jnp.float32),
            pltpu.VMEM((8, width), jnp.float32),
            pltpu.VMEM((8, width), jnp.float32),
            pltpu.VMEM((2, 16, width), jnp.float32),
        ],
        name="chain",
    )(near, two_hi, two_lo, three_hi, three_lo, forcing)
    return code


def high_low(array):
    high = array.astype(jnp.bfloat16).astype(jnp.float32)
    return high.astype(jnp.bfloat16), (array - high).astype(jnp.bfloat16)


def factor(diag_ref, coupling_ref, lag):
    sensors = diag_ref.shape[0]
    lines = []
    for start in range(0, sensors, 2 * LANES):
        end = min(start + 2 * LANES, sensors)
        lines.append(
            -jnp.dot(
                diag_ref[start:end, :end],
                coupling_ref[lag, :end, :],
                precision=lax.Precision.HIGHEST,
                preferred_element_type=jnp.float32,
            )
        )
    return jnp.concatenate(lines, axis=0)


def turned(square_ref, high_ref, low_ref):
    for row in range(0, high_ref.shape[0], LANES):
        for column in range(0, high_ref.shape[1], LANES):
            tile = square_ref[column : column + LANES, row : row + LANES].T
            high, low = high_low(tile)
            high_ref[row : row + LANES, column : column + LANES] = high
            low_ref[row : row + LANES, column : column + LANES] = low


def near_kernel(diag_ref, coupling_ref, near_ref, high_ref, low_ref, square_ref):
    sensors = diag_ref.shape[0]
    near_ref[...] = jnp.zeros_like(near_ref)
    square_ref[...] = jnp.zeros_like(square_ref)
    near_ref[0, :, :sensors] = factor(diag_ref, coupling_ref, 0)
    second = factor(diag_ref, coupling_ref, 1)
    near_ref[1, :, :sensors] = second
    square_ref[:sensors, :sensors] = second
    turned(square_ref, high_ref, low_ref)


def far_kernel(diag_ref, coupling_ref, high_ref, low_ref, square_ref):
    sensors = diag_ref.shape[0]
    square_ref[...] = jnp.zeros_like(square_ref)
    square_ref[:sensors, :sensors] = factor(diag_ref, coupling_ref, 0)
    turned(square_ref, high_ref, low_ref)


def prepare_near(diag_inverse, coupling, width):
    sensors = diag_inverse.shape[0]
    part = jax.ShapeDtypeStruct((2 * LANES, width), jnp.bfloat16)
    return pl.pallas_call(
        near_kernel,
        out_shape=(jax.ShapeDtypeStruct((2, sensors, width), jnp.float32), part, part),
        in_specs=[
            pl.BlockSpec((sensors, sensors), lambda _: (0, 0)),
            pl.BlockSpec((2, sensors, sensors), lambda _: (0, 0, 0)),
        ],
        out_specs=[
            pl.BlockSpec((2, sensors, width), lambda _: (0, 0, 0)),
            pl.BlockSpec((2 * LANES, width), lambda _: (0, 0)),
            pl.BlockSpec((2 * LANES, width), lambda _: (0, 0)),
        ],
        grid=(1,),
        scratch_shapes=[pltpu.VMEM((width, width), jnp.float32)],
        cost_estimate=pl.CostEstimate(
            flops=12 * 2 * sensors**3, bytes_accessed=16 * sensors**2, transcendentals=0
        ),
        name="near_factors",
    )(diag_inverse, coupling)


def prepare_far(diag_inverse, coupling, width):
    sensors = diag_inverse.shape[0]
    part = jax.ShapeDtypeStruct((width, width), jnp.bfloat16)
    return pl.pallas_call(
        far_kernel,
        out_shape=(part, part),
        in_specs=[
            pl.BlockSpec((sensors, sensors), lambda _: (0, 0)),
            pl.BlockSpec((1, sensors, sensors), lambda _: (2, 0, 0)),
        ],
        out_specs=[pl.BlockSpec((width, width), lambda _: (0, 0))] * 2,
        grid=(1,),
        scratch_shapes=[pltpu.VMEM((width, width), jnp.float32)],
        cost_estimate=pl.CostEstimate(
            flops=12 * sensors**3, bytes_accessed=12 * sensors**2, transcendentals=0
        ),
        name="far_factors",
    )(diag_inverse, coupling)


def predict_kernel(offsets_ref, source_ref, kernel_ref, code_ref, total_ref):
    steps, samples, cols = code_ref.shape[1], source_ref.shape[1], source_ref.shape[2]
    sensors = kernel_ref.shape[1]
    lag = pl.program_id(0)
    window = source_ref[pl.ds(REACH - 1 - offsets_ref[lag], steps)]
    window = window.reshape(steps * samples, cols)

    @pl.when(lag == 0)
    def first():
        total_ref[...] = jnp.zeros_like(total_ref)

    for start in range(0, sensors, 2 * LANES):
        end = min(start + 2 * LANES, sensors)
        product = lax.dot_general(
            window,
            kernel_ref[0, start:end, :],
            (((1,), (1,)), ((), ())),
            preferred_element_type=jnp.float32,
        )
        for at in range(start, end, LANES):
            size = min(LANES, end - at)
            piece = product[:, at - start : at - start + size]
            total_ref[at // LANES, :, :size] = total_ref[at // LANES, :, :size] + piece

    @pl.when(lag == pl.num_programs(0) - 1)
    def last():
        def several(group, unused):
            for member in range(4):
                sample = 4 * group + member
                rows = jnp.concatenate(
                    [
                        total_ref[c, pl.ds(sample, steps, stride=samples), :]
                        for c in range(total_ref.shape[0])
                    ],
                    axis=1,
                )
                code_ref[sample] = coded_with_grade(rows, sensors)
            return unused

        lax.fori_loop(0, samples // 4, several, 0)


def predict(source, kernel, lag_offsets):
    lag_count, sensors, cols = kernel.shape
    span, samples, unused_cols = source.shape
    steps = span - (REACH - 1)
    width = -(-sensors // LANES) * LANES
    return pl.pallas_call(
        predict_kernel,
        out_shape=jax.ShapeDtypeStruct((samples, steps, width), jnp.int16),
        in_specs=[
            pl.BlockSpec(memory_space=pltpu.SMEM),
            pl.BlockSpec((span, samples, cols), lambda lag: (0, 0, 0)),
            pl.BlockSpec((1, sensors, cols), lambda lag: (lag, 0, 0)),
        ],
        out_specs=pl.BlockSpec((samples, steps, width), lambda lag: (0, 0, 0)),
        grid=(lag_count,),
        scratch_shapes=[pltpu.VMEM((width // LANES, steps * samples, LANES), jnp.float32)],
        cost_estimate=pl.CostEstimate(
            flops=2 * steps * samples * lag_count * cols * sensors,
            bytes_accessed=2 * lag_count * cols * sensors,
            transcendentals=0,
        ),
        name="predict",
    )(lag_offsets, source, kernel)


def forcing_kernel(place_ref, code_ref, observed_ref, diag_ref, forcing_ref):
    sensors = diag_ref.shape[0]
    copies, steps, unused, width = forcing_ref.shape
    total = None
    for part in range(code_ref.shape[0]):
        code = code_ref[part].astype(jnp.int32).astype(jnp.float32)
        term = code * scale_of(code[:, sensors : sensors + 1])
        total = term if total is None else total + term
    misfit = observed_ref[0].astype(jnp.float32) - total[:, :sensors]
    rows = lax.dot_general(
        misfit,
        diag_ref[...],
        (((1,), (1,)), ((), ())),
        precision=lax.Precision.HIGHEST,
        preferred_element_type=jnp.float32,
    )
    rows = jnp.concatenate([rows, jnp.zeros((steps, width - sensors), jnp.float32)], axis=1)
    for copy in range(copies):
        for step in range(steps):
            forcing_ref[copy, step] = rows[step : step + 1]


def force(code, observed, diag_inverse, place, copies, width):
    parts, steps, wide = code.shape
    sensors = diag_inverse.shape[0]
    return pl.pallas_call(
        forcing_kernel,
        out_shape=jax.ShapeDtypeStruct((copies, steps, 1, width), jnp.float32),
        grid_spec=pltpu.PrefetchScalarGridSpec(
            num_scalar_prefetch=1,
            grid=(1,),
            in_specs=[
                pl.BlockSpec((parts, steps, wide), lambda i, place: (0, 0, 0)),
                pl.BlockSpec((1, steps, sensors), lambda i, place: (place[0], 0, 0)),
                pl.BlockSpec((sensors, sensors), lambda i, place: (0, 0)),
            ],
            out_specs=pl.BlockSpec((copies, steps, 1, width), lambda i, place: (0, 0, 0, 0)),
        ),
        name="forcing",
    )(place, code, observed, diag_inverse)


def per_device(params, kernel, lag_offsets, observed, diag_inverse, coupling):
    samples, step_count, col_count = params.shape
    lag_count, unused_cols, sensors = kernel.shape
    width = -(-sensors // LANES) * LANES
    group = lax.axis_size("param")
    share = samples // group
    by_step = jnp.swapaxes(params, 0, 1)
    rim = from_behind(by_step[step_count - (REACH - 1) :], "tm", 1)
    near = prepare_near(diag_inverse, coupling, width)
    rim, near = lax.optimization_barrier((rim, near))
    code = predict(
        jnp.concatenate([rim, by_step], axis=0), jnp.swapaxes(kernel, 1, 2), lag_offsets
    )
    code = code.reshape(group, share, step_count, width)
    code = lax.all_to_all(code, "param", 0, 0, tiled=True)
    blocks = lax.axis_size("tm")
    first = lax.axis_index("param").astype(jnp.int32) * share
    forced = [
        force(code[:, s], observed, diag_inverse, (first + s).reshape(1), blocks, width)
        for s in range(share)
    ]
    forced, coupling = lax.optimization_barrier((jnp.stack(forced, axis=1), coupling))
    every = lax.all_to_all(forced, "tm", 0, 0, tiled=True)
    factors = (*near, *prepare_far(diag_inverse, coupling, width))
    every = jnp.moveaxis(every, 0, 1).reshape(share, -1, 1, width)
    code = [run_chain(step_count, group, *factors, every[s]) for s in range(share)]
    code = lax.all_to_all(jnp.stack(code, axis=1), "param", 0, 0, tiled=True)
    code = code.reshape(samples, step_count, width)
    grade = code[..., sensors : sensors + 1].astype(jnp.float32)
    return code[..., :sensors].astype(jnp.float32) * scale_of(grade)


def solution(mesh):
    in_specs = (P(None, "tm", "param"), P(None, "param", None), P(), P(None, "tm", None), P(), P())
    out_specs = P(None, "tm", None)
    return jax.shard_map(
        per_device, mesh=mesh, in_specs=in_specs, out_specs=out_specs, check_vma=False
    )
```

```python
import functools

import jax
import jax.numpy as jnp
from jax import lax
from jax.experimental import pallas as pl
from jax.experimental.pallas import tpu as pltpu
from jax.sharding import PartitionSpec as P

REACH = 12
LANES = 128
LEVELS = 32700.0
OCTAVE = 64.0
TINY = 1e-37


def from_behind(block, axis, distance):
    devices = range(lax.axis_size(axis))
    route = [(i - distance, i) for i in devices if i - distance in devices]
    return lax.ppermute(block, axis, route)


def grade_of(rows):
    largest = jnp.maximum(jnp.max(jnp.abs(rows), axis=-1, keepdims=True), TINY)
    return jnp.ceil(jnp.log2(largest) * OCTAVE)


def coded(rows, grade):
    return jnp.round(rows * (LEVELS * jnp.exp2(grade * (-1.0 / OCTAVE))))


def scale_of(grade):
    return jnp.exp2(grade * (1.0 / OCTAVE)) * (1.0 / LEVELS)


def coded_with_grade(rows, place):
    grade = grade_of(rows)
    lane = lax.broadcasted_iota(jnp.int32, rows.shape, 1)
    code = jnp.where(lane == place, grade, coded(rows, grade))
    return code.astype(jnp.int32).astype(jnp.int16)


def row_chunks(rows):
    return [(start, min(LANES, rows - start)) for start in range(0, rows, LANES)]


def chain_kernel(
    block, sensors, near_ref, two_hi, two_lo, three_hi, three_lo, forcing_ref,
    code_ref, solved_ref, later_ref, carry_ref, even_ref, odd_ref, far_ref,
):
    width = near_ref.shape[2]
    pieces = list(range(width // LANES))
    reach = two_hi.shape[0]
    rest = [c for c in pieces if c * LANES >= reach]
    for ref in (later_ref, carry_ref, even_ref, odd_ref):
        ref[...] = jnp.zeros_like(ref)
    dot = functools.partial(jnp.dot, preferred_element_type=jnp.float32)

    def lanes(piece):
        return slice(piece * LANES, (piece + 1) * LANES)

    def wide(row):
        return jnp.broadcast_to(row, (8, LANES))

    def pair(turn, unused):
        diagonal = lax.broadcasted_iota(jnp.int32, (LANES, LANES), 0) == lax.broadcasted_iota(
            jnp.int32, (LANES, LANES), 1
        )
        row_id = lax.broadcasted_iota(jnp.int32, (16, LANES), 0)
        split = []
        for c in pieces:
            older = jnp.concatenate([even_ref[:, lanes(c)]] * 2, axis=0)
            newer = jnp.concatenate([odd_ref[:, lanes(c)]] * 2, axis=0)
            both = jnp.where(row_id < 2, older, jnp.where(row_id < 4, newer, 0.0))
            high = both.astype(jnp.bfloat16).astype(jnp.float32)
            split.append(
                jnp.where((row_id == 0) | (row_id == 2), high, both - high).astype(jnp.bfloat16)
            )
        operand = jnp.concatenate(split, axis=1)
        front = operand[:, :reach]
        far_ref[0] = dot(front, two_hi[...]) + dot(front, two_lo[...])
        far_ref[1] = dot(operand, three_hi[...]) + dot(operand, three_lo[...])

        for half in range(2):
            t = 2 * turn + half
            prev_ref, new_ref = ((odd_ref, even_ref), (even_ref, odd_ref))[half]
            behind = [prev_ref[:, lanes(c)] for c in pieces]
            for piece, (start, rows) in enumerate(row_chunks(sensors)):
                sums = []
                for row in range(start, start + rows, 8):
                    total = later_ref[row : row + 8, :]
                    for c in pieces:
                        total = total + near_ref[0, row : row + 8, lanes(c)] * behind[c]
                    sums.append(total)
                column = jnp.sum(jnp.concatenate(sums, axis=0), axis=1, keepdims=True)
                line = jnp.sum(jnp.where(diagonal[:rows], column, 0.0), axis=0, keepdims=True)
                base = wide(forcing_ref[t, :, lanes(piece)])
                if half == 0:
                    base = base + wide(carry_ref[0:1, lanes(piece)])
                else:
                    base = base + (
                        wide(far_ref[1, 0:1, lanes(piece)]) + wide(far_ref[1, 1:2, lanes(piece)])
                    )
                base = base + (
                    wide(far_ref[0, 2 * half : 2 * half + 1, lanes(piece)])
                    + wide(far_ref[0, 2 * half + 1 : 2 * half + 2, lanes(piece)])
                )
                solved = wide(line) + base
                new_ref[:, lanes(piece)] = solved
                solved_ref[lax.rem(t, block), :, lanes(piece)] = solved[0:1]
            gate = jnp.minimum(jnp.abs(sums[-1]), 0.0)
            behind = {c: prev_ref[:, lanes(c)] + gate for c in rest}
            for start in range(0, sensors, 8):
                total = None
                for c in rest:
                    term = near_ref[1, start : start + 8, lanes(c)] * behind[c]
                    total = term if total is None else total + term
                later_ref[start : start + 8, :] = total
        carry_ref[0:1, :] = far_ref[1, 2:3] + far_ref[1, 3:4]
        return unused

    turns = (lax.axis_index("tm") + 1) * (block // 2)
    def several(group, unused):
        for member in range(4):
            unused = pair(4 * group + member, unused)
        return unused

    lax.fori_loop(0, turns // 4, several, 0)
    own = jnp.concatenate([solved_ref[row] for row in range(block)], axis=0)
    code = coded_with_grade(own, sensors)
    for copy in range(code_ref.shape[0]):
        code_ref[copy] = code


def run_chain(block, copies, near, two_hi, two_lo, three_hi, three_lo, forcing):
    unused_lags, sensors, width = near.shape
    steps = forcing.shape[0]
    code, unused_rows = pl.pallas_call(
        functools.partial(chain_kernel, block, sensors),
        out_shape=(
            jax.ShapeDtypeStruct((copies, block, width), jnp.int16),
            jax.ShapeDtypeStruct((block, 1, width), jnp.float32),
        ),
        in_specs=[pl.BlockSpec(memory_space=pltpu.VMEM)] * 6,
        out_specs=[pl.BlockSpec(memory_space=pltpu.VMEM)] * 2,
        scratch_shapes=[
            pltpu.VMEM((sensors, LANES), jnp.float32),
            pltpu.VMEM((8, width), jnp.float32),
            pltpu.VMEM((8, width), jnp.float32),
            pltpu.VMEM((8, width), jnp.float32),
            pltpu.VMEM((2, 16, width), jnp.float32),
        ],
        name="chain",
    )(near, two_hi, two_lo, three_hi, three_lo, forcing)
    return code


def high_low(array):
    high = array.astype(jnp.bfloat16).astype(jnp.float32)
    return high.astype(jnp.bfloat16), (array - high).astype(jnp.bfloat16)


def factor(diag_ref, coupling_ref, lag):
    sensors = diag_ref.shape[0]
    lines = []
    for start in range(0, sensors, 2 * LANES):
        end = min(start + 2 * LANES, sensors)
        lines.append(
            -jnp.dot(
                diag_ref[start:end, :end],
                coupling_ref[lag, :end, :],
                precision=lax.Precision.HIGHEST,
                preferred_element_type=jnp.float32,
            )
        )
    return jnp.concatenate(lines, axis=0)


def turned(square_ref, high_ref, low_ref):
    for row in range(0, high_ref.shape[0], LANES):
        for column in range(0, high_ref.shape[1], LANES):
            tile = square_ref[column : column + LANES, row : row + LANES].T
            high, low = high_low(tile)
            high_ref[row : row + LANES, column : column + LANES] = high
            low_ref[row : row + LANES, column : column + LANES] = low


def near_kernel(diag_ref, coupling_ref, near_ref, high_ref, low_ref, square_ref):
    sensors = diag_ref.shape[0]
    near_ref[...] = jnp.zeros_like(near_ref)
    square_ref[...] = jnp.zeros_like(square_ref)
    near_ref[0, :, :sensors] = factor(diag_ref, coupling_ref, 0)
    second = factor(diag_ref, coupling_ref, 1)
    near_ref[1, :, :sensors] = second
    square_ref[:sensors, :sensors] = second
    turned(square_ref, high_ref, low_ref)


def far_kernel(diag_ref, coupling_ref, high_ref, low_ref, square_ref):
    sensors = diag_ref.shape[0]
    square_ref[...] = jnp.zeros_like(square_ref)
    square_ref[:sensors, :sensors] = factor(diag_ref, coupling_ref, 0)
    turned(square_ref, high_ref, low_ref)


def prepare_near(diag_inverse, coupling, width):
    sensors = diag_inverse.shape[0]
    part = jax.ShapeDtypeStruct((2 * LANES, width), jnp.bfloat16)
    return pl.pallas_call(
        near_kernel,
        out_shape=(jax.ShapeDtypeStruct((2, sensors, width), jnp.float32), part, part),
        in_specs=[
            pl.BlockSpec((sensors, sensors), lambda _: (0, 0)),
            pl.BlockSpec((2, sensors, sensors), lambda _: (0, 0, 0)),
        ],
        out_specs=[
            pl.BlockSpec((2, sensors, width), lambda _: (0, 0, 0)),
            pl.BlockSpec((2 * LANES, width), lambda _: (0, 0)),
            pl.BlockSpec((2 * LANES, width), lambda _: (0, 0)),
        ],
        grid=(1,),
        scratch_shapes=[pltpu.VMEM((width, width), jnp.float32)],
        cost_estimate=pl.CostEstimate(
            flops=12 * 2 * sensors**3, bytes_accessed=16 * sensors**2, transcendentals=0
        ),
        name="near_factors",
    )(diag_inverse, coupling)


def prepare_far(diag_inverse, coupling, width):
    sensors = diag_inverse.shape[0]
    part = jax.ShapeDtypeStruct((width, width), jnp.bfloat16)
    return pl.pallas_call(
        far_kernel,
        out_shape=(part, part),
        in_specs=[
            pl.BlockSpec((sensors, sensors), lambda _: (0, 0)),
            pl.BlockSpec((1, sensors, sensors), lambda _: (2, 0, 0)),
        ],
        out_specs=[pl.BlockSpec((width, width), lambda _: (0, 0))] * 2,
        grid=(1,),
        scratch_shapes=[pltpu.VMEM((width, width), jnp.float32)],
        cost_estimate=pl.CostEstimate(
            flops=12 * sensors**3, bytes_accessed=12 * sensors**2, transcendentals=0
        ),
        name="far_factors",
    )(diag_inverse, coupling)


def predict_kernel(offsets_ref, source_ref, kernel_hbm, code_ref, kernel_ref, total_ref, arrived):
    samples, cols = source_ref.shape[1:]
    steps = code_ref.shape[1]
    lag_count, sensors, unused = kernel_ref.shape

    def fetch(lag):
        return pltpu.make_async_copy(kernel_hbm.at[lag], kernel_ref.at[lag], arrived.at[lag])

    for lag in range(lag_count):
        fetch(lag).start()
    total_ref[...] = jnp.zeros_like(total_ref)

    def add(lag, unused):
        fetch(lag).wait()
        window = source_ref[pl.ds(REACH - 1 - offsets_ref[lag], steps)]
        window = window.reshape(steps * samples, cols)
        for start in range(0, sensors, 2 * LANES):
            end = min(start + 2 * LANES, sensors)
            product = lax.dot_general(
                window,
                kernel_ref[lag, start:end, :],
                (((1,), (1,)), ((), ())),
                preferred_element_type=jnp.float32,
            )
            for at in range(start, end, LANES):
                size = min(LANES, end - at)
                piece = product[:, at - start : at - start + size]
                total_ref[at // LANES, :, :size] = total_ref[at // LANES, :, :size] + piece
        return unused

    lax.fori_loop(0, lag_count, add, 0)

    def several(group, unused):
        for member in range(4):
            sample = 4 * group + member
            rows = jnp.concatenate(
                [
                    total_ref[c, pl.ds(sample, steps, stride=samples), :]
                    for c in range(total_ref.shape[0])
                ],
                axis=1,
            )
            code_ref[sample] = coded_with_grade(rows, sensors)
        return unused

    lax.fori_loop(0, samples // 4, several, 0)


def predict(source, kernel, lag_offsets):
    lag_count, sensors, cols = kernel.shape
    span, samples, unused_cols = source.shape
    steps = span - (REACH - 1)
    width = -(-sensors // LANES) * LANES
    return pl.pallas_call(
        predict_kernel,
        out_shape=jax.ShapeDtypeStruct((samples, steps, width), jnp.int16),
        in_specs=[
            pl.BlockSpec(memory_space=pltpu.SMEM),
            pl.BlockSpec(memory_space=pltpu.VMEM),
            pl.BlockSpec(memory_space=pl.ANY),
        ],
        out_specs=pl.BlockSpec(memory_space=pltpu.VMEM),
        scratch_shapes=[
            pltpu.VMEM((lag_count, sensors, cols), jnp.bfloat16),
            pltpu.VMEM((width // LANES, steps * samples, LANES), jnp.float32),
            pltpu.SemaphoreType.DMA((lag_count,)),
        ],
        cost_estimate=pl.CostEstimate(
            flops=2 * steps * samples * lag_count * cols * sensors,
            bytes_accessed=2 * lag_count * cols * sensors,
            transcendentals=0,
        ),
        name="predict",
    )(lag_offsets, source, kernel)


def forcing_kernel(place_ref, code_ref, observed_ref, diag_ref, forcing_ref):
    sensors = diag_ref.shape[0]
    copies, steps, unused, width = forcing_ref.shape
    total = None
    for part in range(code_ref.shape[0]):
        code = code_ref[part].astype(jnp.int32).astype(jnp.float32)
        term = code * scale_of(code[:, sensors : sensors + 1])
        total = term if total is None else total + term
    misfit = observed_ref[0].astype(jnp.float32) - total[:, :sensors]
    rows = lax.dot_general(
        misfit,
        diag_ref[...],
        (((1,), (1,)), ((), ())),
        precision=lax.Precision.HIGHEST,
        preferred_element_type=jnp.float32,
    )
    rows = jnp.concatenate([rows, jnp.zeros((steps, width - sensors), jnp.float32)], axis=1)
    for copy in range(copies):
        for step in range(steps):
            forcing_ref[copy, step] = rows[step : step + 1]


def force(code, observed, diag_inverse, place, copies, width):
    parts, steps, wide = code.shape
    sensors = diag_inverse.shape[0]
    return pl.pallas_call(
        forcing_kernel,
        out_shape=jax.ShapeDtypeStruct((copies, steps, 1, width), jnp.float32),
        grid_spec=pltpu.PrefetchScalarGridSpec(
            num_scalar_prefetch=1,
            grid=(1,),
            in_specs=[
                pl.BlockSpec((parts, steps, wide), lambda i, place: (0, 0, 0)),
                pl.BlockSpec((1, steps, sensors), lambda i, place: (place[0], 0, 0)),
                pl.BlockSpec((sensors, sensors), lambda i, place: (0, 0)),
            ],
            out_specs=pl.BlockSpec((copies, steps, 1, width), lambda i, place: (0, 0, 0, 0)),
        ),
        name="forcing",
    )(place, code, observed, diag_inverse)


def per_device(params, kernel, lag_offsets, observed, diag_inverse, coupling):
    samples, step_count, col_count = params.shape
    lag_count, unused_cols, sensors = kernel.shape
    width = -(-sensors // LANES) * LANES
    group = lax.axis_size("param")
    share = samples // group
    by_step = jnp.swapaxes(params, 0, 1)
    rim = from_behind(by_step[step_count - (REACH - 1) :], "tm", 1)
    near = prepare_near(diag_inverse, coupling, width)
    rim, near = lax.optimization_barrier((rim, near))
    code = predict(
        jnp.concatenate([rim, by_step], axis=0), jnp.swapaxes(kernel, 1, 2), lag_offsets
    )
    code = code.reshape(group, share, step_count, width)
    first = lax.axis_index("param").astype(jnp.int32) * share
    code, first = lax.optimization_barrier((code, first))
    code = lax.all_to_all(code, "param", 0, 0, tiled=True)
    blocks = lax.axis_size("tm")
    forced = [
        force(code[:, s], observed, diag_inverse, (first + s).reshape(1), blocks, width)
        for s in range(share)
    ]
    forced, coupling = lax.optimization_barrier((jnp.stack(forced, axis=1), coupling))
    every = lax.all_to_all(forced, "tm", 0, 0, tiled=True)
    factors = (*near, *prepare_far(diag_inverse, coupling, width))
    every = jnp.moveaxis(every, 0, 1).reshape(share, -1, 1, width)
    code = [run_chain(step_count, group, *factors, every[s]) for s in range(share)]
    code = lax.all_to_all(jnp.stack(code, axis=1), "param", 0, 0, tiled=True)
    code = code.reshape(samples, step_count, width)
    grade = code[..., sensors : sensors + 1].astype(jnp.float32)
    return code[..., :sensors].astype(jnp.float32) * scale_of(grade)


def solution(mesh):
    in_specs = (P(None, "tm", "param"), P(None, "param", None), P(), P(None, "tm", None), P(), P())
    out_specs = P(None, "tm", None)
    return jax.shard_map(
        per_device, mesh=mesh, in_specs=in_specs, out_specs=out_specs, check_vma=False
    )
```

```python
import functools

import jax
import jax.numpy as jnp
from jax import lax
from jax.experimental import pallas as pl
from jax.experimental.pallas import tpu as pltpu
from jax.sharding import PartitionSpec as P

REACH = 12
LANES = 128
LEVELS = 32700.0
OCTAVE = 64.0
TINY = 1e-37


def from_behind(block, axis, distance):
    devices = range(lax.axis_size(axis))
    route = [(i - distance, i) for i in devices if i - distance in devices]
    return lax.ppermute(block, axis, route)


def grade_of(rows):
    largest = jnp.maximum(jnp.max(jnp.abs(rows), axis=-1, keepdims=True), TINY)
    return jnp.ceil(jnp.log2(largest) * OCTAVE)


def coded(rows, grade):
    return jnp.round(rows * (LEVELS * jnp.exp2(grade * (-1.0 / OCTAVE))))


def scale_of(grade):
    return jnp.exp2(grade * (1.0 / OCTAVE)) * (1.0 / LEVELS)


def coded_with_grade(rows, place):
    grade = grade_of(rows)
    lane = lax.broadcasted_iota(jnp.int32, rows.shape, 1)
    code = jnp.where(lane == place, grade, coded(rows, grade))
    return code.astype(jnp.int32).astype(jnp.int16)


def row_chunks(rows):
    return [(start, min(LANES, rows - start)) for start in range(0, rows, LANES)]


def chain_kernel(
    block, sensors, near_ref, two_hi, two_lo, three_hi, three_lo, forcing_ref,
    code_ref, solved_ref, later_ref, carry_ref, even_ref, odd_ref, far_ref,
):
    width = near_ref.shape[2]
    pieces = list(range(width // LANES))
    reach = two_hi.shape[0]
    rest = [c for c in pieces if c * LANES >= reach]
    for ref in (later_ref, carry_ref, even_ref, odd_ref):
        ref[...] = jnp.zeros_like(ref)
    dot = functools.partial(jnp.dot, preferred_element_type=jnp.float32)

    def lanes(piece):
        return slice(piece * LANES, (piece + 1) * LANES)

    def wide(row):
        return jnp.broadcast_to(row, (8, LANES))

    def pair(turn, unused):
        diagonal = lax.broadcasted_iota(jnp.int32, (LANES, LANES), 0) == lax.broadcasted_iota(
            jnp.int32, (LANES, LANES), 1
        )
        row_id = lax.broadcasted_iota(jnp.int32, (16, LANES), 0)
        split = []
        for c in pieces:
            older = jnp.concatenate([even_ref[:, lanes(c)]] * 2, axis=0)
            newer = jnp.concatenate([odd_ref[:, lanes(c)]] * 2, axis=0)
            both = jnp.where(row_id < 2, older, jnp.where(row_id < 4, newer, 0.0))
            high = both.astype(jnp.bfloat16).astype(jnp.float32)
            split.append(
                jnp.where((row_id == 0) | (row_id == 2), high, both - high).astype(jnp.bfloat16)
            )
        operand = jnp.concatenate(split, axis=1)
        front = operand[:, :reach]
        far_ref[0] = dot(front, two_hi[...]) + dot(front, two_lo[...])
        far_ref[1] = dot(operand, three_hi[...]) + dot(operand, three_lo[...])

        for half in range(2):
            t = 2 * turn + half
            prev_ref, new_ref = ((odd_ref, even_ref), (even_ref, odd_ref))[half]
            behind = [prev_ref[:, lanes(c)] for c in pieces]
            for piece, (start, rows) in enumerate(row_chunks(sensors)):
                sums = []
                for row in range(start, start + rows, 8):
                    total = later_ref[row : row + 8, :]
                    for c in pieces:
                        total = total + near_ref[0, row : row + 8, lanes(c)] * behind[c]
                    sums.append(total)
                column = jnp.sum(jnp.concatenate(sums, axis=0), axis=1, keepdims=True)
                line = jnp.sum(jnp.where(diagonal[:rows], column, 0.0), axis=0, keepdims=True)
                base = wide(forcing_ref[t, :, lanes(piece)])
                if half == 0:
                    base = base + wide(carry_ref[0:1, lanes(piece)])
                else:
                    base = base + (
                        wide(far_ref[1, 0:1, lanes(piece)]) + wide(far_ref[1, 1:2, lanes(piece)])
                    )
                base = base + (
                    wide(far_ref[0, 2 * half : 2 * half + 1, lanes(piece)])
                    + wide(far_ref[0, 2 * half + 1 : 2 * half + 2, lanes(piece)])
                )
                solved = wide(line) + base
                new_ref[:, lanes(piece)] = solved
                solved_ref[lax.rem(t, block), :, lanes(piece)] = solved[0:1]
            gate = jnp.minimum(jnp.abs(sums[-1]), 0.0)
            behind = {c: prev_ref[:, lanes(c)] + gate for c in rest}
            for start in range(0, sensors, 8):
                total = None
                for c in rest:
                    term = near_ref[1, start : start + 8, lanes(c)] * behind[c]
                    total = term if total is None else total + term
                later_ref[start : start + 8, :] = total
        carry_ref[0:1, :] = far_ref[1, 2:3] + far_ref[1, 3:4]
        return unused

    turns = (lax.axis_index("tm") + 1) * (block // 2)
    def several(group, unused):
        for member in range(4):
            unused = pair(4 * group + member, unused)
        return unused

    lax.fori_loop(0, turns // 4, several, 0)
    own = jnp.concatenate([solved_ref[row] for row in range(block)], axis=0)
    code = coded_with_grade(own, sensors)
    for copy in range(code_ref.shape[0]):
        code_ref[copy] = code


def run_chain(block, copies, near, two_hi, two_lo, three_hi, three_lo, forcing):
    unused_lags, sensors, width = near.shape
    steps = forcing.shape[0]
    code, unused_rows = pl.pallas_call(
        functools.partial(chain_kernel, block, sensors),
        out_shape=(
            jax.ShapeDtypeStruct((copies, block, width), jnp.int16),
            jax.ShapeDtypeStruct((block, 1, width), jnp.float32),
        ),
        in_specs=[pl.BlockSpec(memory_space=pltpu.VMEM)] * 6,
        out_specs=[pl.BlockSpec(memory_space=pltpu.VMEM)] * 2,
        scratch_shapes=[
            pltpu.VMEM((sensors, LANES), jnp.float32),
            pltpu.VMEM((8, width), jnp.float32),
            pltpu.VMEM((8, width), jnp.float32),
            pltpu.VMEM((8, width), jnp.float32),
            pltpu.VMEM((2, 16, width), jnp.float32),
        ],
        name="chain",
    )(near, two_hi, two_lo, three_hi, three_lo, forcing)
    return code


def high_low(array):
    high = array.astype(jnp.bfloat16).astype(jnp.float32)
    return high.astype(jnp.bfloat16), (array - high).astype(jnp.bfloat16)


def factor(diag_ref, coupling_ref, lag):
    sensors = diag_ref.shape[0]
    lines = []
    for start in range(0, sensors, 2 * LANES):
        end = min(start + 2 * LANES, sensors)
        lines.append(
            -jnp.dot(
                diag_ref[start:end, :end],
                coupling_ref[lag, :end, :],
                precision=lax.Precision.HIGHEST,
                preferred_element_type=jnp.float32,
            )
        )
    return jnp.concatenate(lines, axis=0)


def turned(square_ref, high_ref, low_ref):
    for row in range(0, high_ref.shape[0], LANES):
        for column in range(0, high_ref.shape[1], LANES):
            tile = square_ref[column : column + LANES, row : row + LANES].T
            high, low = high_low(tile)
            high_ref[row : row + LANES, column : column + LANES] = high
            low_ref[row : row + LANES, column : column + LANES] = low


def near_kernel(diag_ref, coupling_ref, near_ref, high_ref, low_ref, square_ref):
    sensors = diag_ref.shape[0]
    near_ref[...] = jnp.zeros_like(near_ref)
    square_ref[...] = jnp.zeros_like(square_ref)
    near_ref[0, :, :sensors] = factor(diag_ref, coupling_ref, 0)
    second = factor(diag_ref, coupling_ref, 1)
    near_ref[1, :, :sensors] = second
    square_ref[:sensors, :sensors] = second
    turned(square_ref, high_ref, low_ref)


def far_kernel(diag_ref, coupling_ref, high_ref, low_ref, square_ref):
    sensors = diag_ref.shape[0]
    square_ref[...] = jnp.zeros_like(square_ref)
    square_ref[:sensors, :sensors] = factor(diag_ref, coupling_ref, 0)
    turned(square_ref, high_ref, low_ref)


def prepare_near(diag_inverse, coupling, width):
    sensors = diag_inverse.shape[0]
    part = jax.ShapeDtypeStruct((2 * LANES, width), jnp.bfloat16)
    return pl.pallas_call(
        near_kernel,
        out_shape=(jax.ShapeDtypeStruct((2, sensors, width), jnp.float32), part, part),
        in_specs=[
            pl.BlockSpec((sensors, sensors), lambda _: (0, 0)),
            pl.BlockSpec((2, sensors, sensors), lambda _: (0, 0, 0)),
        ],
        out_specs=[
            pl.BlockSpec((2, sensors, width), lambda _: (0, 0, 0)),
            pl.BlockSpec((2 * LANES, width), lambda _: (0, 0)),
            pl.BlockSpec((2 * LANES, width), lambda _: (0, 0)),
        ],
        grid=(1,),
        scratch_shapes=[pltpu.VMEM((width, width), jnp.float32)],
        cost_estimate=pl.CostEstimate(
            flops=12 * 2 * sensors**3, bytes_accessed=16 * sensors**2, transcendentals=0
        ),
        name="near_factors",
    )(diag_inverse, coupling)


def prepare_far(diag_inverse, coupling, width):
    sensors = diag_inverse.shape[0]
    part = jax.ShapeDtypeStruct((width, width), jnp.bfloat16)
    return pl.pallas_call(
        far_kernel,
        out_shape=(part, part),
        in_specs=[
            pl.BlockSpec((sensors, sensors), lambda _: (0, 0)),
            pl.BlockSpec((1, sensors, sensors), lambda _: (2, 0, 0)),
        ],
        out_specs=[pl.BlockSpec((width, width), lambda _: (0, 0))] * 2,
        grid=(1,),
        scratch_shapes=[pltpu.VMEM((width, width), jnp.float32)],
        cost_estimate=pl.CostEstimate(
            flops=12 * sensors**3, bytes_accessed=12 * sensors**2, transcendentals=0
        ),
        name="far_factors",
    )(diag_inverse, coupling)


def predict_kernel(
    offsets_ref, source_ref, kernel_hbm, code_ref, own_ref, kernel_ref, total_ref, arrived
):
    samples, cols = source_ref.shape[1:]
    steps = code_ref.shape[1]
    lag_count, sensors, unused = kernel_ref.shape

    def fetch(lag):
        return pltpu.make_async_copy(kernel_hbm.at[lag], kernel_ref.at[lag], arrived.at[lag])

    for lag in range(lag_count):
        fetch(lag).start()
    total_ref[...] = jnp.zeros_like(total_ref)

    def add(lag, unused):
        fetch(lag).wait()
        window = source_ref[pl.ds(REACH - 1 - offsets_ref[lag], steps)]
        window = window.reshape(steps * samples, cols)
        for start in range(0, sensors, 2 * LANES):
            end = min(start + 2 * LANES, sensors)
            product = lax.dot_general(
                window,
                kernel_ref[lag, start:end, :],
                (((1,), (1,)), ((), ())),
                preferred_element_type=jnp.float32,
            )
            for at in range(start, end, LANES):
                size = min(LANES, end - at)
                piece = product[:, at - start : at - start + size]
                total_ref[at // LANES, :, :size] = total_ref[at // LANES, :, :size] + piece
        return unused

    lax.fori_loop(0, lag_count, add, 0)

    core = lax.rem(lax.axis_index("param"), 2)

    def rows_of(sample):
        return jnp.concatenate(
            [
                total_ref[c, pl.ds(sample, steps, stride=samples), :]
                for c in range(total_ref.shape[0])
            ],
            axis=1,
        )

    def several(group, unused):
        for member in range(4):
            pair = 4 * group + member
            code_ref[pair] = coded_with_grade(rows_of(2 * pair + 1 - core), sensors)
            own_ref[pair] = rows_of(2 * pair + core)
        return unused

    lax.fori_loop(0, samples // 8, several, 0)


def predict(source, kernel, lag_offsets):
    lag_count, sensors, cols = kernel.shape
    span, samples, unused_cols = source.shape
    steps = span - (REACH - 1)
    width = -(-sensors // LANES) * LANES
    return pl.pallas_call(
        predict_kernel,
        out_shape=(
            jax.ShapeDtypeStruct((samples // 2, steps, width), jnp.int16),
            jax.ShapeDtypeStruct((samples // 2, steps, width), jnp.float32),
        ),
        in_specs=[
            pl.BlockSpec(memory_space=pltpu.SMEM),
            pl.BlockSpec(memory_space=pltpu.VMEM),
            pl.BlockSpec(memory_space=pl.ANY),
        ],
        out_specs=[pl.BlockSpec(memory_space=pltpu.VMEM)] * 2,
        scratch_shapes=[
            pltpu.VMEM((lag_count, sensors, cols), jnp.bfloat16),
            pltpu.VMEM((width // LANES, steps * samples, LANES), jnp.float32),
            pltpu.SemaphoreType.DMA((lag_count,)),
        ],
        cost_estimate=pl.CostEstimate(
            flops=2 * steps * samples * lag_count * cols * sensors,
            bytes_accessed=2 * lag_count * cols * sensors,
            transcendentals=0,
        ),
        name="predict",
    )(lag_offsets, source, kernel)


def decoded(code, sensors):
    values = code.astype(jnp.int32).astype(jnp.float32)
    return values * scale_of(values[:, sensors : sensors + 1])


def merge_kernel(sensors, own_ref, code_ref, merged_ref):
    lane = lax.broadcasted_iota(jnp.int32, own_ref.shape[1:], 1)

    def several(group, unused):
        for member in range(4):
            pair = 4 * group + member
            other = jnp.where(lane < sensors, decoded(code_ref[pair], sensors), 0.0)
            merged_ref[pair] = coded_with_grade(own_ref[pair] + other, sensors)
        return unused

    lax.fori_loop(0, own_ref.shape[0] // 4, several, 0)


def merge(own, code, sensors):
    return pl.pallas_call(
        functools.partial(merge_kernel, sensors),
        out_shape=jax.ShapeDtypeStruct(code.shape, code.dtype),
        in_specs=[pl.BlockSpec(memory_space=pltpu.VMEM)] * 2,
        out_specs=pl.BlockSpec(memory_space=pltpu.VMEM),
        name="merge",
    )(own, code)


def decode_kernel(own_ref, other_ref, out_ref):
    sensors = out_ref.shape[3]
    core = lax.rem(lax.axis_index("param"), 2)

    def one(pair, unused):
        out_ref[pair, core] = decoded(own_ref[pair], sensors)[:, :sensors]
        out_ref[pair, 1 - core] = decoded(other_ref[pair], sensors)[:, :sensors]
        return unused

    lax.fori_loop(0, own_ref.shape[0], one, 0, unroll=4)


def decode(own, other, sensors):
    pairs, steps, unused = own.shape
    out = pl.pallas_call(
        decode_kernel,
        out_shape=jax.ShapeDtypeStruct((pairs, 2, steps, sensors), jnp.float32),
        in_specs=[pl.BlockSpec(memory_space=pltpu.VMEM)] * 2,
        out_specs=pl.BlockSpec(memory_space=pltpu.VMEM),
        name="decode",
    )(own, other)
    return out.reshape(2 * pairs, steps, sensors)


def forcing_kernel(place_ref, code_ref, observed_ref, diag_ref, forcing_ref):
    sensors = diag_ref.shape[0]
    copies, steps, unused, width = forcing_ref.shape
    total = None
    for part in range(code_ref.shape[0]):
        code = code_ref[part].astype(jnp.int32).astype(jnp.float32)
        term = code * scale_of(code[:, sensors : sensors + 1])
        total = term if total is None else total + term
    misfit = observed_ref[0].astype(jnp.float32) - total[:, :sensors]
    rows = lax.dot_general(
        misfit,
        diag_ref[...],
        (((1,), (1,)), ((), ())),
        precision=lax.Precision.HIGHEST,
        preferred_element_type=jnp.float32,
    )
    rows = jnp.concatenate([rows, jnp.zeros((steps, width - sensors), jnp.float32)], axis=1)
    for copy in range(copies):
        for step in range(steps):
            forcing_ref[copy, step] = rows[step : step + 1]


def force(code, observed, diag_inverse, place, copies, width):
    parts, steps, wide = code.shape
    sensors = diag_inverse.shape[0]
    return pl.pallas_call(
        forcing_kernel,
        out_shape=jax.ShapeDtypeStruct((copies, steps, 1, width), jnp.float32),
        grid_spec=pltpu.PrefetchScalarGridSpec(
            num_scalar_prefetch=1,
            grid=(1,),
            in_specs=[
                pl.BlockSpec((parts, steps, wide), lambda i, place: (0, 0, 0)),
                pl.BlockSpec((1, steps, sensors), lambda i, place: (place[0], 0, 0)),
                pl.BlockSpec((sensors, sensors), lambda i, place: (0, 0)),
            ],
            out_specs=pl.BlockSpec((copies, steps, 1, width), lambda i, place: (0, 0, 0, 0)),
        ),
        name="forcing",
    )(place, code, observed, diag_inverse)


def per_device(params, kernel, lag_offsets, observed, diag_inverse, coupling):
    samples, step_count, col_count = params.shape
    lag_count, unused_cols, sensors = kernel.shape
    width = -(-sensors // LANES) * LANES
    group = lax.axis_size("param")
    share = samples // group
    by_step = jnp.swapaxes(params, 0, 1)
    rim = from_behind(by_step[step_count - (REACH - 1) :], "tm", 1)
    near = prepare_near(diag_inverse, coupling, width)
    rim, near = lax.optimization_barrier((rim, near))
    assert share == 1
    chips = [list(range(core, group, 2)) for core in range(2)]
    partner = [(i, i ^ 1) for i in range(group)]
    code, own = predict(
        jnp.concatenate([rim, by_step], axis=0), jnp.swapaxes(kernel, 1, 2), lag_offsets
    )
    code = merge(own, lax.ppermute(code, "param", partner), sensors)
    place = lax.axis_index("param").astype(jnp.int32).reshape(1)
    code, place = lax.optimization_barrier((code, place))
    code = lax.all_to_all(code, "param", 0, 0, tiled=True, axis_index_groups=chips)
    blocks = lax.axis_size("tm")
    forced = force(code, observed, diag_inverse, place, blocks, width)
    forced, coupling = lax.optimization_barrier((forced, coupling))
    every = lax.all_to_all(forced, "tm", 0, 0, tiled=True)
    factors = (*near, *prepare_far(diag_inverse, coupling, width))
    code = run_chain(step_count, group // 2, *factors, every.reshape(-1, 1, width))
    code = lax.all_to_all(code, "param", 0, 0, tiled=True, axis_index_groups=chips)
    return decode(code, lax.ppermute(code, "param", partner), sensors)


def solution(mesh):
    in_specs = (P(None, "tm", "param"), P(None, "param", None), P(), P(None, "tm", None), P(), P())
    out_specs = P(None, "tm", None)
    return jax.shard_map(
        per_device, mesh=mesh, in_specs=in_specs, out_specs=out_specs, check_vma=False
    )
```

```python
import functools

import jax
import jax.numpy as jnp
from jax import lax
from jax.experimental import pallas as pl
from jax.experimental.pallas import tpu as pltpu
from jax.sharding import PartitionSpec as P

REACH = 12
AHEAD = 3
LANES = 128
LEVELS = 32700.0
OCTAVE = 64.0
TINY = 1e-37


def from_behind(block, axis, distance):
    devices = range(lax.axis_size(axis))
    route = [(i - distance, i) for i in devices if i - distance in devices]
    return lax.ppermute(block, axis, route)


def grade_of(rows):
    largest = jnp.maximum(jnp.max(jnp.abs(rows), axis=-1, keepdims=True), TINY)
    return jnp.ceil(jnp.log2(largest) * OCTAVE)


def coded(rows, grade):
    return jnp.round(rows * (LEVELS * jnp.exp2(grade * (-1.0 / OCTAVE))))


def scale_of(grade):
    return jnp.exp2(grade * (1.0 / OCTAVE)) * (1.0 / LEVELS)


def coded_with_grade(rows, place):
    grade = grade_of(rows)
    lane = lax.broadcasted_iota(jnp.int32, rows.shape, 1)
    code = jnp.where(lane == place, grade, coded(rows, grade))
    return code.astype(jnp.int32).astype(jnp.int16)


def row_chunks(rows):
    return [(start, min(LANES, rows - start)) for start in range(0, rows, LANES)]


def chain_kernel(
    block, sensors, near_ref, two_hi, two_lo, three_hi, three_lo, forcing_ref,
    code_ref, solved_ref, later_ref, carry_ref, even_ref, odd_ref, far_ref,
):
    width = near_ref.shape[2]
    pieces = list(range(width // LANES))
    reach = two_hi.shape[0]
    rest = [c for c in pieces if c * LANES >= reach]
    for ref in (later_ref, carry_ref, even_ref, odd_ref):
        ref[...] = jnp.zeros_like(ref)
    dot = functools.partial(jnp.dot, preferred_element_type=jnp.float32)

    def lanes(piece):
        return slice(piece * LANES, (piece + 1) * LANES)

    def wide(row):
        return jnp.broadcast_to(row, (8, LANES))

    def pair(turn, unused):
        diagonal = lax.broadcasted_iota(jnp.int32, (LANES, LANES), 0) == lax.broadcasted_iota(
            jnp.int32, (LANES, LANES), 1
        )
        row_id = lax.broadcasted_iota(jnp.int32, (16, LANES), 0)
        split = []
        for c in pieces:
            older = jnp.concatenate([even_ref[:, lanes(c)]] * 2, axis=0)
            newer = jnp.concatenate([odd_ref[:, lanes(c)]] * 2, axis=0)
            both = jnp.where(row_id < 2, older, jnp.where(row_id < 4, newer, 0.0))
            high = both.astype(jnp.bfloat16).astype(jnp.float32)
            split.append(
                jnp.where((row_id == 0) | (row_id == 2), high, both - high).astype(jnp.bfloat16)
            )
        operand = jnp.concatenate(split, axis=1)
        front = operand[:, :reach]
        far_ref[0] = dot(front, two_hi[...]) + dot(front, two_lo[...])
        far_ref[1] = dot(operand, three_hi[...]) + dot(operand, three_lo[...])

        for half in range(2):
            t = 2 * turn + half
            prev_ref, new_ref = ((odd_ref, even_ref), (even_ref, odd_ref))[half]
            behind = [prev_ref[:, lanes(c)] for c in pieces]
            for piece, (start, rows) in enumerate(row_chunks(sensors)):
                sums = []
                for row in range(start, start + rows, 8):
                    total = later_ref[row : row + 8, :]
                    for c in pieces:
                        total = total + near_ref[0, row : row + 8, lanes(c)] * behind[c]
                    sums.append(total)
                column = jnp.sum(jnp.concatenate(sums, axis=0), axis=1, keepdims=True)
                line = jnp.sum(jnp.where(diagonal[:rows], column, 0.0), axis=0, keepdims=True)
                base = wide(forcing_ref[t, :, lanes(piece)])
                if half == 0:
                    base = base + wide(carry_ref[0:1, lanes(piece)])
                else:
                    base = base + (
                        wide(far_ref[1, 0:1, lanes(piece)]) + wide(far_ref[1, 1:2, lanes(piece)])
                    )
                base = base + (
                    wide(far_ref[0, 2 * half : 2 * half + 1, lanes(piece)])
                    + wide(far_ref[0, 2 * half + 1 : 2 * half + 2, lanes(piece)])
                )
                solved = wide(line) + base
                new_ref[:, lanes(piece)] = solved
                solved_ref[lax.rem(t, block), :, lanes(piece)] = solved[0:1]
            gate = jnp.minimum(jnp.abs(sums[-1]), 0.0)
            behind = {c: prev_ref[:, lanes(c)] + gate for c in rest}
            for start in range(0, sensors, 8):
                total = None
                for c in rest:
                    term = near_ref[1, start : start + 8, lanes(c)] * behind[c]
                    total = term if total is None else total + term
                later_ref[start : start + 8, :] = total
        carry_ref[0:1, :] = far_ref[1, 2:3] + far_ref[1, 3:4]
        return unused

    turns = (lax.axis_index("tm") + 1) * (block // 2)
    def several(group, unused):
        for member in range(4):
            unused = pair(4 * group + member, unused)
        return unused

    lax.fori_loop(0, turns // 4, several, 0)
    own = jnp.concatenate([solved_ref[row] for row in range(block)], axis=0)
    code = coded_with_grade(own, sensors)
    for copy in range(code_ref.shape[0]):
        code_ref[copy] = code


def run_chain(block, copies, near, two_hi, two_lo, three_hi, three_lo, forcing):
    unused_lags, sensors, width = near.shape
    steps = forcing.shape[0]
    code, unused_rows = pl.pallas_call(
        functools.partial(chain_kernel, block, sensors),
        out_shape=(
            jax.ShapeDtypeStruct((copies, block, width), jnp.int16),
            jax.ShapeDtypeStruct((block, 1, width), jnp.float32),
        ),
        in_specs=[pl.BlockSpec(memory_space=pltpu.VMEM)] * 6,
        out_specs=[pl.BlockSpec(memory_space=pltpu.VMEM)] * 2,
        scratch_shapes=[
            pltpu.VMEM((sensors, LANES), jnp.float32),
            pltpu.VMEM((8, width), jnp.float32),
            pltpu.VMEM((8, width), jnp.float32),
            pltpu.VMEM((8, width), jnp.float32),
            pltpu.VMEM((2, 16, width), jnp.float32),
        ],
        name="chain",
    )(near, two_hi, two_lo, three_hi, three_lo, forcing)
    return code


def high_low(array):
    high = array.astype(jnp.bfloat16).astype(jnp.float32)
    return high.astype(jnp.bfloat16), (array - high).astype(jnp.bfloat16)


def factor(diag_ref, coupling_ref, lag):
    sensors = diag_ref.shape[0]
    lines = []
    for start in range(0, sensors, 2 * LANES):
        end = min(start + 2 * LANES, sensors)
        lines.append(
            -jnp.dot(
                diag_ref[start:end, :end],
                coupling_ref[lag, :end, :],
                precision=lax.Precision.HIGHEST,
                preferred_element_type=jnp.float32,
            )
        )
    return jnp.concatenate(lines, axis=0)


def turned(square_ref, high_ref, low_ref):
    for row in range(0, high_ref.shape[0], LANES):
        for column in range(0, high_ref.shape[1], LANES):
            tile = square_ref[column : column + LANES, row : row + LANES].T
            high, low = high_low(tile)
            high_ref[row : row + LANES, column : column + LANES] = high
            low_ref[row : row + LANES, column : column + LANES] = low


def near_kernel(diag_ref, coupling_ref, near_ref, high_ref, low_ref, square_ref):
    sensors = diag_ref.shape[0]
    near_ref[...] = jnp.zeros_like(near_ref)
    square_ref[...] = jnp.zeros_like(square_ref)
    near_ref[0, :, :sensors] = factor(diag_ref, coupling_ref, 0)
    second = factor(diag_ref, coupling_ref, 1)
    near_ref[1, :, :sensors] = second
    square_ref[:sensors, :sensors] = second
    turned(square_ref, high_ref, low_ref)


def far_kernel(diag_ref, coupling_ref, high_ref, low_ref, square_ref):
    sensors = diag_ref.shape[0]
    square_ref[...] = jnp.zeros_like(square_ref)
    square_ref[:sensors, :sensors] = factor(diag_ref, coupling_ref, 0)
    turned(square_ref, high_ref, low_ref)


def prepare_near(diag_inverse, coupling, width):
    sensors = diag_inverse.shape[0]
    part = jax.ShapeDtypeStruct((2 * LANES, width), jnp.bfloat16)
    return pl.pallas_call(
        near_kernel,
        out_shape=(jax.ShapeDtypeStruct((2, sensors, width), jnp.float32), part, part),
        in_specs=[
            pl.BlockSpec((sensors, sensors), lambda _: (0, 0)),
            pl.BlockSpec((2, sensors, sensors), lambda _: (0, 0, 0)),
        ],
        out_specs=[
            pl.BlockSpec((2, sensors, width), lambda _: (0, 0, 0)),
            pl.BlockSpec((2 * LANES, width), lambda _: (0, 0)),
            pl.BlockSpec((2 * LANES, width), lambda _: (0, 0)),
        ],
        grid=(1,),
        scratch_shapes=[pltpu.VMEM((width, width), jnp.float32)],
        cost_estimate=pl.CostEstimate(
            flops=12 * 2 * sensors**3, bytes_accessed=16 * sensors**2, transcendentals=0
        ),
        name="near_factors",
    )(diag_inverse, coupling)


def prepare_far(diag_inverse, coupling, width):
    sensors = diag_inverse.shape[0]
    part = jax.ShapeDtypeStruct((width, width), jnp.bfloat16)
    return pl.pallas_call(
        far_kernel,
        out_shape=(part, part),
        in_specs=[
            pl.BlockSpec((sensors, sensors), lambda _: (0, 0)),
            pl.BlockSpec((1, sensors, sensors), lambda _: (2, 0, 0)),
        ],
        out_specs=[pl.BlockSpec((width, width), lambda _: (0, 0))] * 2,
        grid=(1,),
        scratch_shapes=[pltpu.VMEM((width, width), jnp.float32)],
        cost_estimate=pl.CostEstimate(
            flops=12 * sensors**3, bytes_accessed=12 * sensors**2, transcendentals=0
        ),
        name="far_factors",
    )(diag_inverse, coupling)


def predict_kernel(
    offsets_ref, rim_hbm, steps_hbm, kernel_hbm, code_ref, own_ref,
    source_ref, kernel_ref, total_ref, arrived, here,
):
    samples, cols = source_ref.shape[1:]
    steps = code_ref.shape[1]
    lag_count, sensors, unused = kernel_ref.shape

    def fetch(lag):
        return pltpu.make_async_copy(kernel_hbm.at[lag], kernel_ref.at[lag], arrived.at[lag])

    rim_rows = rim_hbm.shape[0]
    inputs = [
        pltpu.make_async_copy(steps_hbm, source_ref.at[rim_rows:], here.at[0]),
        pltpu.make_async_copy(rim_hbm, source_ref.at[:rim_rows], here.at[1]),
    ]
    for copy in inputs:
        copy.start()
    for lag in range(AHEAD):
        fetch(lag).start()
    total_ref[...] = jnp.zeros_like(total_ref)
    for copy in inputs:
        copy.wait()

    def add(lag, unused):
        fetch(lag).wait()

        @pl.when(lag + AHEAD < lag_count)
        def more():
            fetch(lag + AHEAD).start()

        window = source_ref[pl.ds(REACH - 1 - offsets_ref[lag], steps)]
        window = window.reshape(steps * samples, cols)
        for start in range(0, sensors, 2 * LANES):
            end = min(start + 2 * LANES, sensors)
            product = lax.dot_general(
                window,
                kernel_ref[lag, start:end, :],
                (((1,), (1,)), ((), ())),
                preferred_element_type=jnp.float32,
            )
            for at in range(start, end, LANES):
                size = min(LANES, end - at)
                piece = product[:, at - start : at - start + size]
                total_ref[at // LANES, :, :size] = total_ref[at // LANES, :, :size] + piece
        return unused

    lax.fori_loop(0, lag_count, add, 0)

    core = lax.rem(lax.axis_index("param"), 2)

    def rows_of(sample):
        return jnp.concatenate(
            [
                total_ref[c, pl.ds(sample, steps, stride=samples), :]
                for c in range(total_ref.shape[0])
            ],
            axis=1,
        )

    def several(group, unused):
        for member in range(4):
            pair = 4 * group + member
            code_ref[pair] = coded_with_grade(rows_of(2 * pair + 1 - core), sensors)
            own_ref[pair] = rows_of(2 * pair + core)
        return unused

    lax.fori_loop(0, samples // 8, several, 0)


def predict(rim, by_step, kernel, lag_offsets):
    lag_count, sensors, cols = kernel.shape
    steps, samples, unused_cols = by_step.shape
    width = -(-sensors // LANES) * LANES
    return pl.pallas_call(
        predict_kernel,
        out_shape=(
            jax.ShapeDtypeStruct((samples // 2, steps, width), jnp.int16),
            jax.ShapeDtypeStruct((samples // 2, steps, width), jnp.float32),
        ),
        in_specs=[
            pl.BlockSpec(memory_space=pltpu.SMEM),
            pl.BlockSpec(memory_space=pl.ANY),
            pl.BlockSpec(memory_space=pl.ANY),
            pl.BlockSpec(memory_space=pl.ANY),
        ],
        out_specs=[pl.BlockSpec(memory_space=pltpu.VMEM)] * 2,
        scratch_shapes=[
            pltpu.VMEM((rim.shape[0] + steps, samples, cols), jnp.bfloat16),
            pltpu.VMEM((lag_count, sensors, cols), jnp.bfloat16),
            pltpu.VMEM((width // LANES, steps * samples, LANES), jnp.float32),
            pltpu.SemaphoreType.DMA((lag_count,)),
            pltpu.SemaphoreType.DMA((2,)),
        ],
        cost_estimate=pl.CostEstimate(
            flops=2 * steps * samples * lag_count * cols * sensors,
            bytes_accessed=2 * lag_count * cols * sensors,
            transcendentals=0,
        ),
        name="predict",
    )(lag_offsets, rim, by_step, kernel)


def decoded(code, sensors):
    values = code.astype(jnp.int32).astype(jnp.float32)
    return values * scale_of(values[:, sensors : sensors + 1])


def merge_kernel(sensors, own_ref, code_ref, merged_ref):
    lane = lax.broadcasted_iota(jnp.int32, own_ref.shape[1:], 1)

    for pair in range(own_ref.shape[0]):
        other = jnp.where(lane < sensors, decoded(code_ref[pair], sensors), 0.0)
        merged_ref[pair] = coded_with_grade(own_ref[pair] + other, sensors)


def merge(own, code, sensors):
    return pl.pallas_call(
        functools.partial(merge_kernel, sensors),
        out_shape=jax.ShapeDtypeStruct(code.shape, code.dtype),
        in_specs=[pl.BlockSpec((4, *own.shape[1:]), lambda i: (i, 0, 0))] * 2,
        out_specs=pl.BlockSpec((4, *own.shape[1:]), lambda i: (i, 0, 0)),
        grid=(own.shape[0] // 4,),
        name="merge",
    )(own, code)


def decode_kernel(own_ref, other_ref, out_ref):
    sensors = out_ref.shape[3]
    core = lax.rem(lax.axis_index("param"), 2)

    for pair in range(own_ref.shape[0]):
        out_ref[pair, core] = decoded(own_ref[pair], sensors)[:, :sensors]
        out_ref[pair, 1 - core] = decoded(other_ref[pair], sensors)[:, :sensors]


def decode(own, other, sensors):
    pairs, steps, unused = own.shape
    out = pl.pallas_call(
        decode_kernel,
        out_shape=jax.ShapeDtypeStruct((pairs, 2, steps, sensors), jnp.float32),
        in_specs=[pl.BlockSpec((4, *own.shape[1:]), lambda i: (i, 0, 0))] * 2,
        out_specs=pl.BlockSpec((4, 2, steps, sensors), lambda i: (i, 0, 0, 0)),
        grid=(pairs // 4,),
        name="decode",
    )(own, other)
    return out.reshape(2 * pairs, steps, sensors)


def forcing_kernel(place_ref, code_ref, observed_ref, diag_ref, forcing_ref):
    sensors = diag_ref.shape[0]
    copies, steps, unused, width = forcing_ref.shape
    total = None
    for part in range(code_ref.shape[0]):
        code = code_ref[part].astype(jnp.int32).astype(jnp.float32)
        term = code * scale_of(code[:, sensors : sensors + 1])
        total = term if total is None else total + term
    misfit = observed_ref[0].astype(jnp.float32) - total[:, :sensors]
    rows = lax.dot_general(
        misfit,
        diag_ref[...],
        (((1,), (1,)), ((), ())),
        precision=lax.Precision.HIGHEST,
        preferred_element_type=jnp.float32,
    )
    rows = jnp.concatenate([rows, jnp.zeros((steps, width - sensors), jnp.float32)], axis=1)
    for copy in range(copies):
        for step in range(steps):
            forcing_ref[copy, step] = rows[step : step + 1]


def force(code, observed, diag_inverse, place, copies, width):
    parts, steps, wide = code.shape
    sensors = diag_inverse.shape[0]
    return pl.pallas_call(
        forcing_kernel,
        out_shape=jax.ShapeDtypeStruct((copies, steps, 1, width), jnp.float32),
        grid_spec=pltpu.PrefetchScalarGridSpec(
            num_scalar_prefetch=1,
            grid=(1,),
            in_specs=[
                pl.BlockSpec((parts, steps, wide), lambda i, place: (0, 0, 0)),
                pl.BlockSpec((1, steps, sensors), lambda i, place: (place[0], 0, 0)),
                pl.BlockSpec((sensors, sensors), lambda i, place: (0, 0)),
            ],
            out_specs=pl.BlockSpec((copies, steps, 1, width), lambda i, place: (0, 0, 0, 0)),
        ),
        name="forcing",
    )(place, code, observed, diag_inverse)


def per_device(params, kernel, lag_offsets, observed, diag_inverse, coupling):
    samples, step_count, col_count = params.shape
    lag_count, unused_cols, sensors = kernel.shape
    width = -(-sensors // LANES) * LANES
    group = lax.axis_size("param")
    share = samples // group
    by_step = jnp.swapaxes(params, 0, 1)
    rim = from_behind(by_step[step_count - (REACH - 1) :], "tm", 1)
    near = prepare_near(diag_inverse, coupling, width)
    rim, near = lax.optimization_barrier((rim, near))
    assert share == 1
    chips = [list(range(core, group, 2)) for core in range(2)]
    partner = [(i, i ^ 1) for i in range(group)]
    code, own = predict(rim, by_step, jnp.swapaxes(kernel, 1, 2), lag_offsets)
    code = merge(own, lax.ppermute(code, "param", partner), sensors)
    place = lax.axis_index("param").astype(jnp.int32).reshape(1)
    code, place = lax.optimization_barrier((code, place))
    code = lax.all_to_all(code, "param", 0, 0, tiled=True, axis_index_groups=chips)
    blocks = lax.axis_size("tm")
    forced = force(code, observed, diag_inverse, place, blocks, width)
    forced, coupling = lax.optimization_barrier((forced, coupling))
    every = lax.all_to_all(forced, "tm", 0, 0, tiled=True)
    factors = (*near, *prepare_far(diag_inverse, coupling, width))
    code = run_chain(step_count, group // 2, *factors, every.reshape(-1, 1, width))
    code = lax.all_to_all(code, "param", 0, 0, tiled=True, axis_index_groups=chips)
    return decode(code, lax.ppermute(code, "param", partner), sensors)


def solution(mesh):
    in_specs = (P(None, "tm", "param"), P(None, "param", None), P(), P(None, "tm", None), P(), P())
    out_specs = P(None, "tm", None)
    return jax.shard_map(
        per_device, mesh=mesh, in_specs=in_specs, out_specs=out_specs, check_vma=False
    )
```

```python
import functools

import jax
import jax.numpy as jnp
from jax import lax
from jax.experimental import pallas as pl
from jax.experimental.pallas import tpu as pltpu
from jax.sharding import PartitionSpec as P

REACH = 12
LANES = 128
LEVELS = 32700.0
OCTAVE = 64.0
TINY = 1e-37


def from_behind(block, axis, distance):
    devices = range(lax.axis_size(axis))
    route = [(i - distance, i) for i in devices if i - distance in devices]
    return lax.ppermute(block, axis, route)


def grade_of(rows):
    largest = jnp.maximum(jnp.max(jnp.abs(rows), axis=-1, keepdims=True), TINY)
    return jnp.ceil(jnp.log2(largest) * OCTAVE)


def coded(rows, grade):
    return jnp.round(rows * (LEVELS * jnp.exp2(grade * (-1.0 / OCTAVE))))


def scale_of(grade):
    return jnp.exp2(grade * (1.0 / OCTAVE)) * (1.0 / LEVELS)


def coded_with_grade(rows, place):
    grade = grade_of(rows)
    lane = lax.broadcasted_iota(jnp.int32, rows.shape, 1)
    code = jnp.where(lane == place, grade, coded(rows, grade))
    return code.astype(jnp.int32).astype(jnp.int16)


def row_chunks(rows):
    return [(start, min(LANES, rows - start)) for start in range(0, rows, LANES)]


def chain_kernel(
    block, sensors, near_ref, two_hi, two_lo, three_hi, three_lo, forcing_ref,
    code_ref, solved_ref, later_ref, carry_ref, even_ref, odd_ref, far_ref,
):
    width = near_ref.shape[2]
    pieces = list(range(width // LANES))
    reach = two_hi.shape[0]
    rest = [c for c in pieces if c * LANES >= reach]
    for ref in (later_ref, carry_ref, even_ref, odd_ref):
        ref[...] = jnp.zeros_like(ref)
    dot = functools.partial(jnp.dot, preferred_element_type=jnp.float32)

    def lanes(piece):
        return slice(piece * LANES, (piece + 1) * LANES)

    def wide(row):
        return jnp.broadcast_to(row, (8, LANES))

    def pair(turn, unused):
        diagonal = lax.broadcasted_iota(jnp.int32, (LANES, LANES), 0) == lax.broadcasted_iota(
            jnp.int32, (LANES, LANES), 1
        )
        row_id = lax.broadcasted_iota(jnp.int32, (16, LANES), 0)
        split = []
        for c in pieces:
            older = jnp.concatenate([even_ref[:, lanes(c)]] * 2, axis=0)
            newer = jnp.concatenate([odd_ref[:, lanes(c)]] * 2, axis=0)
            both = jnp.where(row_id < 2, older, jnp.where(row_id < 4, newer, 0.0))
            high = both.astype(jnp.bfloat16).astype(jnp.float32)
            split.append(
                jnp.where((row_id == 0) | (row_id == 2), high, both - high).astype(jnp.bfloat16)
            )
        operand = jnp.concatenate(split, axis=1)
        front = operand[:, :reach]
        far_ref[0] = dot(front, two_hi[...]) + dot(front, two_lo[...])
        far_ref[1] = dot(operand, three_hi[...]) + dot(operand, three_lo[...])

        for half in range(2):
            t = 2 * turn + half
            prev_ref, new_ref = ((odd_ref, even_ref), (even_ref, odd_ref))[half]
            behind = [prev_ref[:, lanes(c)] for c in pieces]
            for piece, (start, rows) in enumerate(row_chunks(sensors)):
                sums = []
                for row in range(start, start + rows, 8):
                    total = later_ref[row : row + 8, :]
                    for c in pieces:
                        total = total + near_ref[0, row : row + 8, lanes(c)] * behind[c]
                    sums.append(total)
                column = jnp.sum(jnp.concatenate(sums, axis=0), axis=1, keepdims=True)
                line = jnp.sum(jnp.where(diagonal[:rows], column, 0.0), axis=0, keepdims=True)
                base = wide(forcing_ref[t, :, lanes(piece)])
                if half == 0:
                    base = base + wide(carry_ref[0:1, lanes(piece)])
                else:
                    base = base + (
                        wide(far_ref[1, 0:1, lanes(piece)]) + wide(far_ref[1, 1:2, lanes(piece)])
                    )
                base = base + (
                    wide(far_ref[0, 2 * half : 2 * half + 1, lanes(piece)])
                    + wide(far_ref[0, 2 * half + 1 : 2 * half + 2, lanes(piece)])
                )
                solved = wide(line) + base
                new_ref[:, lanes(piece)] = solved
                solved_ref[lax.rem(t, block), :, lanes(piece)] = solved[0:1]
            gate = jnp.minimum(jnp.abs(sums[-1]), 0.0)
            behind = {c: prev_ref[:, lanes(c)] + gate for c in rest}
            for start in range(0, sensors, 8):
                total = None
                for c in rest:
                    term = near_ref[1, start : start + 8, lanes(c)] * behind[c]
                    total = term if total is None else total + term
                later_ref[start : start + 8, :] = total
        carry_ref[0:1, :] = far_ref[1, 2:3] + far_ref[1, 3:4]
        return unused

    turns = (lax.axis_index("tm") + 1) * (block // 2)
    def several(group, unused):
        for member in range(4):
            unused = pair(4 * group + member, unused)
        return unused

    lax.fori_loop(0, turns // 4, several, 0)
    own = jnp.concatenate([solved_ref[row] for row in range(block)], axis=0)
    code = coded_with_grade(own, sensors)
    for copy in range(code_ref.shape[0]):
        code_ref[copy] = code


def run_chain(block, copies, near, two_hi, two_lo, three_hi, three_lo, forcing):
    unused_lags, sensors, width = near.shape
    steps = forcing.shape[0]
    code, unused_rows = pl.pallas_call(
        functools.partial(chain_kernel, block, sensors),
        out_shape=(
            jax.ShapeDtypeStruct((copies, block, width), jnp.int16),
            jax.ShapeDtypeStruct((block, 1, width), jnp.float32),
        ),
        in_specs=[pl.BlockSpec(memory_space=pltpu.VMEM)] * 6,
        out_specs=[pl.BlockSpec(memory_space=pltpu.VMEM)] * 2,
        scratch_shapes=[
            pltpu.VMEM((sensors, LANES), jnp.float32),
            pltpu.VMEM((8, width), jnp.float32),
            pltpu.VMEM((8, width), jnp.float32),
            pltpu.VMEM((8, width), jnp.float32),
            pltpu.VMEM((2, 16, width), jnp.float32),
        ],
        name="chain",
        compiler_params=pltpu.CompilerParams(vmem_limit_bytes=12 << 20),
    )(near, two_hi, two_lo, three_hi, three_lo, forcing)
    return code


def high_low(array):
    high = array.astype(jnp.bfloat16).astype(jnp.float32)
    return high.astype(jnp.bfloat16), (array - high).astype(jnp.bfloat16)


def factor(diag_ref, coupling_ref, lag):
    sensors = diag_ref.shape[0]
    lines = []
    for start in range(0, sensors, 2 * LANES):
        end = min(start + 2 * LANES, sensors)
        lines.append(
            -jnp.dot(
                diag_ref[start:end, :end],
                coupling_ref[lag, :end, :],
                precision=lax.Precision.HIGHEST,
                preferred_element_type=jnp.float32,
            )
        )
    return jnp.concatenate(lines, axis=0)


def turned(square_ref, high_ref, low_ref):
    for row in range(0, high_ref.shape[0], LANES):
        for column in range(0, high_ref.shape[1], LANES):
            tile = square_ref[column : column + LANES, row : row + LANES].T
            high, low = high_low(tile)
            high_ref[row : row + LANES, column : column + LANES] = high
            low_ref[row : row + LANES, column : column + LANES] = low


def near_kernel(diag_ref, coupling_ref, near_ref, high_ref, low_ref, square_ref):
    sensors = diag_ref.shape[0]
    near_ref[...] = jnp.zeros_like(near_ref)
    square_ref[...] = jnp.zeros_like(square_ref)
    near_ref[0, :, :sensors] = factor(diag_ref, coupling_ref, 0)
    second = factor(diag_ref, coupling_ref, 1)
    near_ref[1, :, :sensors] = second
    square_ref[:sensors, :sensors] = second
    turned(square_ref, high_ref, low_ref)


def far_kernel(diag_ref, coupling_ref, high_ref, low_ref, square_ref):
    sensors = diag_ref.shape[0]
    square_ref[...] = jnp.zeros_like(square_ref)
    square_ref[:sensors, :sensors] = factor(diag_ref, coupling_ref, 0)
    turned(square_ref, high_ref, low_ref)


def prepare_near(diag_inverse, coupling, width):
    sensors = diag_inverse.shape[0]
    part = jax.ShapeDtypeStruct((2 * LANES, width), jnp.bfloat16)
    return pl.pallas_call(
        near_kernel,
        out_shape=(jax.ShapeDtypeStruct((2, sensors, width), jnp.float32), part, part),
        in_specs=[
            pl.BlockSpec((sensors, sensors), lambda _: (0, 0)),
            pl.BlockSpec((2, sensors, sensors), lambda _: (0, 0, 0)),
        ],
        out_specs=[
            pl.BlockSpec((2, sensors, width), lambda _: (0, 0, 0)),
            pl.BlockSpec((2 * LANES, width), lambda _: (0, 0)),
            pl.BlockSpec((2 * LANES, width), lambda _: (0, 0)),
        ],
        grid=(1,),
        scratch_shapes=[pltpu.VMEM((width, width), jnp.float32)],
        cost_estimate=pl.CostEstimate(
            flops=12 * 2 * sensors**3, bytes_accessed=16 * sensors**2, transcendentals=0
        ),
        name="near_factors",
        compiler_params=pltpu.CompilerParams(vmem_limit_bytes=18 << 20),
    )(diag_inverse, coupling)


def prepare_far(diag_inverse, coupling, width):
    sensors = diag_inverse.shape[0]
    part = jax.ShapeDtypeStruct((width, width), jnp.bfloat16)
    return pl.pallas_call(
        far_kernel,
        out_shape=(part, part),
        in_specs=[
            pl.BlockSpec((sensors, sensors), lambda _: (0, 0)),
            pl.BlockSpec((1, sensors, sensors), lambda _: (2, 0, 0)),
        ],
        out_specs=[pl.BlockSpec((width, width), lambda _: (0, 0))] * 2,
        grid=(1,),
        scratch_shapes=[pltpu.VMEM((width, width), jnp.float32)],
        cost_estimate=pl.CostEstimate(
            flops=12 * sensors**3, bytes_accessed=12 * sensors**2, transcendentals=0
        ),
        name="far_factors",
        compiler_params=pltpu.CompilerParams(vmem_limit_bytes=14 << 20),
    )(diag_inverse, coupling)


def predict_kernel(
    offsets_ref, source_ref, kernel_hbm, code_ref, own_ref, kernel_ref, total_ref, arrived
):
    samples, cols = source_ref.shape[1:]
    steps = code_ref.shape[1]
    lag_count, sensors, unused = kernel_ref.shape

    def fetch(lag):
        return pltpu.make_async_copy(kernel_hbm.at[lag], kernel_ref.at[lag], arrived.at[lag])

    for lag in range(lag_count):
        fetch(lag).start()
    total_ref[...] = jnp.zeros_like(total_ref)

    def add(lag, unused):
        fetch(lag).wait()
        window = source_ref[pl.ds(REACH - 1 - offsets_ref[lag], steps)]
        window = window.reshape(steps * samples, cols)
        for start in range(0, sensors, 2 * LANES):
            end = min(start + 2 * LANES, sensors)
            product = lax.dot_general(
                window,
                kernel_ref[lag, start:end, :],
                (((1,), (1,)), ((), ())),
                preferred_element_type=jnp.float32,
            )
            for at in range(start, end, LANES):
                size = min(LANES, end - at)
                piece = product[:, at - start : at - start + size]
                total_ref[at // LANES, :, :size] = total_ref[at // LANES, :, :size] + piece
        return unused

    lax.fori_loop(0, lag_count, add, 0)

    core = lax.rem(lax.axis_index("param"), 2)

    def rows_of(sample):
        return jnp.concatenate(
            [
                total_ref[c, pl.ds(sample, steps, stride=samples), :]
                for c in range(total_ref.shape[0])
            ],
            axis=1,
        )

    def several(group, unused):
        for member in range(4):
            pair = 4 * group + member
            code_ref[pair] = coded_with_grade(rows_of(2 * pair + 1 - core), sensors)
            own_ref[pair] = rows_of(2 * pair + core)
        return unused

    lax.fori_loop(0, samples // 8, several, 0)


def predict(source, kernel, lag_offsets):
    lag_count, sensors, cols = kernel.shape
    span, samples, unused_cols = source.shape
    steps = span - (REACH - 1)
    width = -(-sensors // LANES) * LANES
    return pl.pallas_call(
        predict_kernel,
        out_shape=(
            jax.ShapeDtypeStruct((samples // 2, steps, width), jnp.int16),
            jax.ShapeDtypeStruct((samples // 2, steps, width), jnp.float32),
        ),
        in_specs=[
            pl.BlockSpec(memory_space=pltpu.SMEM),
            pl.BlockSpec(memory_space=pltpu.VMEM),
            pl.BlockSpec(memory_space=pl.ANY),
        ],
        out_specs=[pl.BlockSpec(memory_space=pltpu.VMEM)] * 2,
        scratch_shapes=[
            pltpu.VMEM((lag_count, sensors, cols), jnp.bfloat16),
            pltpu.VMEM((width // LANES, steps * samples, LANES), jnp.float32),
            pltpu.SemaphoreType.DMA((lag_count,)),
        ],
        cost_estimate=pl.CostEstimate(
            flops=2 * steps * samples * lag_count * cols * sensors,
            bytes_accessed=2 * lag_count * cols * sensors,
            transcendentals=0,
        ),
        name="predict",
        compiler_params=pltpu.CompilerParams(vmem_limit_bytes=14 << 20),
    )(lag_offsets, source, kernel)


def decoded(code, sensors):
    values = code.astype(jnp.int32).astype(jnp.float32)
    return values * scale_of(values[:, sensors : sensors + 1])


def merge_kernel(sensors, own_ref, code_ref, merged_ref):
    lane = lax.broadcasted_iota(jnp.int32, own_ref.shape[1:], 1)

    def several(group, unused):
        for member in range(4):
            pair = 4 * group + member
            other = jnp.where(lane < sensors, decoded(code_ref[pair], sensors), 0.0)
            merged_ref[pair] = coded_with_grade(own_ref[pair] + other, sensors)
        return unused

    lax.fori_loop(0, own_ref.shape[0] // 4, several, 0)


def merge(own, code, sensors):
    return pl.pallas_call(
        functools.partial(merge_kernel, sensors),
        out_shape=jax.ShapeDtypeStruct(code.shape, code.dtype),
        in_specs=[pl.BlockSpec(memory_space=pltpu.VMEM)] * 2,
        out_specs=pl.BlockSpec(memory_space=pltpu.VMEM),
        name="merge",
        compiler_params=pltpu.CompilerParams(vmem_limit_bytes=4 << 20),
    )(own, code)


def decode_kernel(own_ref, other_ref, out_ref):
    sensors = out_ref.shape[3]
    core = lax.rem(lax.axis_index("param"), 2)

    def one(pair, unused):
        out_ref[pair, core] = decoded(own_ref[pair], sensors)[:, :sensors]
        out_ref[pair, 1 - core] = decoded(other_ref[pair], sensors)[:, :sensors]
        return unused

    lax.fori_loop(0, own_ref.shape[0], one, 0, unroll=4)


def decode(own, other, sensors):
    pairs, steps, unused = own.shape
    out = pl.pallas_call(
        decode_kernel,
        out_shape=jax.ShapeDtypeStruct((pairs, 2, steps, sensors), jnp.float32),
        in_specs=[pl.BlockSpec(memory_space=pltpu.VMEM)] * 2,
        out_specs=pl.BlockSpec(memory_space=pltpu.VMEM),
        name="decode",
        compiler_params=pltpu.CompilerParams(vmem_limit_bytes=6 << 20),
    )(own, other)
    return out.reshape(2 * pairs, steps, sensors)


def forcing_kernel(place_ref, code_ref, observed_ref, diag_ref, forcing_ref):
    sensors = diag_ref.shape[0]
    copies, steps, unused, width = forcing_ref.shape
    total = None
    for part in range(code_ref.shape[0]):
        code = code_ref[part].astype(jnp.int32).astype(jnp.float32)
        term = code * scale_of(code[:, sensors : sensors + 1])
        total = term if total is None else total + term
    misfit = observed_ref[0].astype(jnp.float32) - total[:, :sensors]
    rows = lax.dot_general(
        misfit,
        diag_ref[...],
        (((1,), (1,)), ((), ())),
        precision=lax.Precision.HIGHEST,
        preferred_element_type=jnp.float32,
    )
    rows = jnp.concatenate([rows, jnp.zeros((steps, width - sensors), jnp.float32)], axis=1)
    for copy in range(copies):
        for step in range(steps):
            forcing_ref[copy, step] = rows[step : step + 1]


def force(code, observed, diag_inverse, place, copies, width):
    parts, steps, wide = code.shape
    sensors = diag_inverse.shape[0]
    return pl.pallas_call(
        forcing_kernel,
        out_shape=jax.ShapeDtypeStruct((copies, steps, 1, width), jnp.float32),
        grid_spec=pltpu.PrefetchScalarGridSpec(
            num_scalar_prefetch=1,
            grid=(1,),
            in_specs=[
                pl.BlockSpec((parts, steps, wide), lambda i, place: (0, 0, 0)),
                pl.BlockSpec((1, steps, sensors), lambda i, place: (place[0], 0, 0)),
                pl.BlockSpec((sensors, sensors), lambda i, place: (0, 0)),
            ],
            out_specs=pl.BlockSpec((copies, steps, 1, width), lambda i, place: (0, 0, 0, 0)),
        ),
        name="forcing",
        compiler_params=pltpu.CompilerParams(vmem_limit_bytes=6 << 20),
    )(place, code, observed, diag_inverse)


def per_device(params, kernel, lag_offsets, observed, diag_inverse, coupling):
    samples, step_count, col_count = params.shape
    lag_count, unused_cols, sensors = kernel.shape
    width = -(-sensors // LANES) * LANES
    group = lax.axis_size("param")
    share = samples // group
    by_step = jnp.swapaxes(params, 0, 1)
    rim = from_behind(by_step[step_count - (REACH - 1) :], "tm", 1)
    near = prepare_near(diag_inverse, coupling, width)
    rim, near = lax.optimization_barrier((rim, near))
    assert share == 1
    chips = [list(range(core, group, 2)) for core in range(2)]
    partner = [(i, i ^ 1) for i in range(group)]
    code, own = predict(
        jnp.concatenate([rim, by_step], axis=0), jnp.swapaxes(kernel, 1, 2), lag_offsets
    )
    code = merge(own, lax.ppermute(code, "param", partner), sensors)
    place = lax.axis_index("param").astype(jnp.int32).reshape(1)
    code, place = lax.optimization_barrier((code, place))
    code = lax.all_to_all(code, "param", 0, 0, tiled=True, axis_index_groups=chips)
    blocks = lax.axis_size("tm")
    forced = force(code, observed, diag_inverse, place, blocks, width)
    forced, coupling = lax.optimization_barrier((forced, coupling))
    every = lax.all_to_all(forced, "tm", 0, 0, tiled=True)
    factors = (*near, *prepare_far(diag_inverse, coupling, width))
    code = run_chain(step_count, group // 2, *factors, every.reshape(-1, 1, width))
    code = lax.all_to_all(code, "param", 0, 0, tiled=True, axis_index_groups=chips)
    return decode(code, lax.ppermute(code, "param", partner), sensors)


def solution(mesh):
    in_specs = (P(None, "tm", "param"), P(None, "param", None), P(), P(None, "tm", None), P(), P())
    out_specs = P(None, "tm", None)
    return jax.shard_map(
        per_device, mesh=mesh, in_specs=in_specs, out_specs=out_specs, check_vma=False
    )
```

```python
import functools

import jax
import jax.numpy as jnp
from jax import lax
from jax.experimental import pallas as pl
from jax.experimental.pallas import tpu as pltpu
from jax.sharding import PartitionSpec as P

REACH = 12
LANES = 128
LEVELS = 32700.0
OCTAVE = 64.0
TINY = 1e-37


def from_behind(block, axis, distance):
    devices = range(lax.axis_size(axis))
    route = [(i - distance, i) for i in devices if i - distance in devices]
    return lax.ppermute(block, axis, route)


def grade_of(rows):
    largest = jnp.maximum(jnp.max(jnp.abs(rows), axis=-1, keepdims=True), TINY)
    return jnp.ceil(jnp.log2(largest) * OCTAVE)


def coded(rows, grade):
    return jnp.round(rows * (LEVELS * jnp.exp2(grade * (-1.0 / OCTAVE))))


def scale_of(grade):
    return jnp.exp2(grade * (1.0 / OCTAVE)) * (1.0 / LEVELS)


def coded_with_grade(rows, place):
    grade = grade_of(rows)
    lane = lax.broadcasted_iota(jnp.int32, rows.shape, 1)
    code = jnp.where(lane == place, grade, coded(rows, grade))
    return code.astype(jnp.int32).astype(jnp.int16)


def row_chunks(rows):
    return [(start, min(LANES, rows - start)) for start in range(0, rows, LANES)]


def chain_kernel(
    block, sensors, near_ref, two_hi, two_lo, three_hi, three_lo, forcing_ref,
    code_ref, solved_ref, later_ref, carry_ref, even_ref, odd_ref, far_ref,
):
    width = near_ref.shape[2]
    pieces = list(range(width // LANES))
    reach = two_hi.shape[0]
    rest = [c for c in pieces if c * LANES >= reach]
    for ref in (later_ref, carry_ref, even_ref, odd_ref):
        ref[...] = jnp.zeros_like(ref)
    dot = functools.partial(jnp.dot, preferred_element_type=jnp.float32)

    def lanes(piece):
        return slice(piece * LANES, (piece + 1) * LANES)

    def wide(row):
        return jnp.broadcast_to(row, (8, LANES))

    def pair(turn, unused):
        diagonal = lax.broadcasted_iota(jnp.int32, (LANES, LANES), 0) == lax.broadcasted_iota(
            jnp.int32, (LANES, LANES), 1
        )
        row_id = lax.broadcasted_iota(jnp.int32, (16, LANES), 0)
        split = []
        for c in pieces:
            older = jnp.concatenate([even_ref[:, lanes(c)]] * 2, axis=0)
            newer = jnp.concatenate([odd_ref[:, lanes(c)]] * 2, axis=0)
            both = jnp.where(row_id < 2, older, jnp.where(row_id < 4, newer, 0.0))
            high = both.astype(jnp.bfloat16).astype(jnp.float32)
            split.append(
                jnp.where((row_id == 0) | (row_id == 2), high, both - high).astype(jnp.bfloat16)
            )
        operand = jnp.concatenate(split, axis=1)
        front = operand[:, :reach]
        far_ref[0] = dot(front, two_hi[...]) + dot(front, two_lo[...])
        far_ref[1] = dot(operand, three_hi[...]) + dot(operand, three_lo[...])

        for half in range(2):
            t = 2 * turn + half
            prev_ref, new_ref = ((odd_ref, even_ref), (even_ref, odd_ref))[half]
            behind = [prev_ref[:, lanes(c)] for c in pieces]
            for piece, (start, rows) in enumerate(row_chunks(sensors)):
                sums = []
                for row in range(start, start + rows, 8):
                    total = later_ref[row : row + 8, :]
                    for c in pieces:
                        total = total + near_ref[0, row : row + 8, lanes(c)] * behind[c]
                    sums.append(total)
                column = jnp.sum(jnp.concatenate(sums, axis=0), axis=1, keepdims=True)
                line = jnp.sum(jnp.where(diagonal[:rows], column, 0.0), axis=0, keepdims=True)
                base = wide(forcing_ref[t, :, lanes(piece)])
                if half == 0:
                    base = base + wide(carry_ref[0:1, lanes(piece)])
                else:
                    base = base + (
                        wide(far_ref[1, 0:1, lanes(piece)]) + wide(far_ref[1, 1:2, lanes(piece)])
                    )
                base = base + (
                    wide(far_ref[0, 2 * half : 2 * half + 1, lanes(piece)])
                    + wide(far_ref[0, 2 * half + 1 : 2 * half + 2, lanes(piece)])
                )
                solved = wide(line) + base
                new_ref[:, lanes(piece)] = solved
                solved_ref[lax.rem(t, block), :, lanes(piece)] = solved[0:1]
            gate = jnp.minimum(jnp.abs(sums[-1]), 0.0)
            behind = {c: prev_ref[:, lanes(c)] + gate for c in rest}
            for start in range(0, sensors, 8):
                total = None
                for c in rest:
                    term = near_ref[1, start : start + 8, lanes(c)] * behind[c]
                    total = term if total is None else total + term
                later_ref[start : start + 8, :] = total
        carry_ref[0:1, :] = far_ref[1, 2:3] + far_ref[1, 3:4]
        return unused

    turns = (lax.axis_index("tm") + 1) * (block // 2)
    def several(group, unused):
        for member in range(4):
            unused = pair(4 * group + member, unused)
        return unused

    lax.fori_loop(0, turns // 4, several, 0)
    own = jnp.concatenate([solved_ref[row] for row in range(block)], axis=0)
    code = coded_with_grade(own, sensors)
    for copy in range(code_ref.shape[0]):
        code_ref[copy] = code


def run_chain(block, copies, near, two_hi, two_lo, three_hi, three_lo, forcing):
    unused_lags, sensors, width = near.shape
    steps = forcing.shape[0]
    code, unused_rows = pl.pallas_call(
        functools.partial(chain_kernel, block, sensors),
        out_shape=(
            jax.ShapeDtypeStruct((copies, block, width), jnp.int16),
            jax.ShapeDtypeStruct((block, 1, width), jnp.float32),
        ),
        in_specs=[pl.BlockSpec(memory_space=pltpu.VMEM)] * 6,
        out_specs=[pl.BlockSpec(memory_space=pltpu.VMEM)] * 2,
        scratch_shapes=[
            pltpu.VMEM((sensors, LANES), jnp.float32),
            pltpu.VMEM((8, width), jnp.float32),
            pltpu.VMEM((8, width), jnp.float32),
            pltpu.VMEM((8, width), jnp.float32),
            pltpu.VMEM((2, 16, width), jnp.float32),
        ],
        name="chain",
    )(near, two_hi, two_lo, three_hi, three_lo, forcing)
    return code


def high_low(array):
    high = array.astype(jnp.bfloat16).astype(jnp.float32)
    return high.astype(jnp.bfloat16), (array - high).astype(jnp.bfloat16)


def factor(diag_ref, coupling_ref, lag):
    sensors = diag_ref.shape[0]
    lines = []
    for start in range(0, sensors, 2 * LANES):
        end = min(start + 2 * LANES, sensors)
        lines.append(
            -jnp.dot(
                diag_ref[start:end, :end],
                coupling_ref[lag, :end, :],
                precision=lax.Precision.HIGHEST,
                preferred_element_type=jnp.float32,
            )
        )
    return jnp.concatenate(lines, axis=0)


def turned(square_ref, high_ref, low_ref):
    for row in range(0, high_ref.shape[0], LANES):
        for column in range(0, high_ref.shape[1], LANES):
            tile = square_ref[column : column + LANES, row : row + LANES].T
            high, low = high_low(tile)
            high_ref[row : row + LANES, column : column + LANES] = high
            low_ref[row : row + LANES, column : column + LANES] = low


def near_kernel(diag_ref, coupling_ref, near_ref, high_ref, low_ref, square_ref):
    sensors = diag_ref.shape[0]
    near_ref[...] = jnp.zeros_like(near_ref)
    square_ref[...] = jnp.zeros_like(square_ref)
    near_ref[0, :, :sensors] = factor(diag_ref, coupling_ref, 0)
    second = factor(diag_ref, coupling_ref, 1)
    near_ref[1, :, :sensors] = second
    square_ref[:sensors, :sensors] = second
    turned(square_ref, high_ref, low_ref)


def far_kernel(diag_ref, coupling_ref, high_ref, low_ref, square_ref):
    sensors = diag_ref.shape[0]
    square_ref[...] = jnp.zeros_like(square_ref)
    square_ref[:sensors, :sensors] = factor(diag_ref, coupling_ref, 0)
    turned(square_ref, high_ref, low_ref)


def prepare_near(diag_inverse, coupling, width):
    sensors = diag_inverse.shape[0]
    part = jax.ShapeDtypeStruct((2 * LANES, width), jnp.bfloat16)
    return pl.pallas_call(
        near_kernel,
        out_shape=(jax.ShapeDtypeStruct((2, sensors, width), jnp.float32), part, part),
        in_specs=[
            pl.BlockSpec((sensors, sensors), lambda _: (0, 0)),
            pl.BlockSpec((2, sensors, sensors), lambda _: (0, 0, 0)),
        ],
        out_specs=[
            pl.BlockSpec((2, sensors, width), lambda _: (0, 0, 0)),
            pl.BlockSpec((2 * LANES, width), lambda _: (0, 0)),
            pl.BlockSpec((2 * LANES, width), lambda _: (0, 0)),
        ],
        grid=(1,),
        scratch_shapes=[pltpu.VMEM((width, width), jnp.float32)],
        cost_estimate=pl.CostEstimate(
            flops=12 * 2 * sensors**3, bytes_accessed=16 * sensors**2, transcendentals=0
        ),
        name="near_factors",
    )(diag_inverse, coupling)


def prepare_far(diag_inverse, coupling, width):
    sensors = diag_inverse.shape[0]
    part = jax.ShapeDtypeStruct((width, width), jnp.bfloat16)
    return pl.pallas_call(
        far_kernel,
        out_shape=(part, part),
        in_specs=[
            pl.BlockSpec((sensors, sensors), lambda _: (0, 0)),
            pl.BlockSpec((1, sensors, sensors), lambda _: (2, 0, 0)),
        ],
        out_specs=[pl.BlockSpec((width, width), lambda _: (0, 0))] * 2,
        grid=(1,),
        scratch_shapes=[pltpu.VMEM((width, width), jnp.float32)],
        cost_estimate=pl.CostEstimate(
            flops=12 * sensors**3, bytes_accessed=12 * sensors**2, transcendentals=0
        ),
        name="far_factors",
    )(diag_inverse, coupling)


def predict_kernel(
    offsets_ref, source_ref, kernel_hbm, code_ref, own_ref, kernel_ref, total_ref, arrived
):
    samples, cols = source_ref.shape[1:]
    steps = code_ref.shape[1]
    lag_count, sensors, unused = kernel_ref.shape

    def fetch(lag):
        return pltpu.make_async_copy(kernel_hbm.at[lag], kernel_ref.at[lag], arrived.at[lag])

    for lag in range(lag_count):
        fetch(lag).start()
    total_ref[...] = jnp.zeros_like(total_ref)

    def add(lag, unused):
        fetch(lag).wait()
        window = source_ref[pl.ds(REACH - 1 - offsets_ref[lag], steps)]
        window = window.reshape(steps * samples, cols)
        for start in range(0, sensors, 2 * LANES):
            end = min(start + 2 * LANES, sensors)
            product = lax.dot_general(
                window,
                kernel_ref[lag, start:end, :],
                (((1,), (1,)), ((), ())),
                preferred_element_type=jnp.float32,
            )
            for at in range(start, end, LANES):
                size = min(LANES, end - at)
                piece = product[:, at - start : at - start + size]
                total_ref[at // LANES, :, :size] = total_ref[at // LANES, :, :size] + piece
        return unused

    lax.fori_loop(0, lag_count, add, 0)

    core = lax.rem(lax.axis_index("param"), 2)

    def rows_of(sample):
        return jnp.concatenate(
            [
                total_ref[c, pl.ds(sample, steps, stride=samples), :]
                for c in range(total_ref.shape[0])
            ],
            axis=1,
        )

    def several(group, unused):
        for member in range(4):
            pair = 4 * group + member
            code_ref[pair] = coded_with_grade(rows_of(2 * pair + 1 - core), sensors)
            own_ref[pair] = rows_of(2 * pair + core)
        return unused

    lax.fori_loop(0, samples // 8, several, 0)


def predict(source, kernel, lag_offsets):
    lag_count, sensors, cols = kernel.shape
    span, samples, unused_cols = source.shape
    steps = span - (REACH - 1)
    width = -(-sensors // LANES) * LANES
    return pl.pallas_call(
        predict_kernel,
        out_shape=(
            jax.ShapeDtypeStruct((samples // 2, steps, width), jnp.int16),
            jax.ShapeDtypeStruct((samples // 2, steps, width), jnp.float32),
        ),
        in_specs=[
            pl.BlockSpec(memory_space=pltpu.SMEM),
            pl.BlockSpec(memory_space=pltpu.VMEM),
            pl.BlockSpec(memory_space=pl.ANY),
        ],
        out_specs=[pl.BlockSpec(memory_space=pltpu.VMEM)] * 2,
        scratch_shapes=[
            pltpu.VMEM((lag_count, sensors, cols), jnp.bfloat16),
            pltpu.VMEM((width // LANES, steps * samples, LANES), jnp.float32),
            pltpu.SemaphoreType.DMA((lag_count,)),
        ],
        cost_estimate=pl.CostEstimate(
            flops=2 * steps * samples * lag_count * cols * sensors,
            bytes_accessed=2 * lag_count * cols * sensors,
            transcendentals=0,
        ),
        name="predict",
    )(lag_offsets, source, kernel)


def decoded(code, sensors):
    values = code.astype(jnp.int32).astype(jnp.float32)
    return values * scale_of(values[:, sensors : sensors + 1])


def merge_kernel(sensors, own_ref, code_ref, merged_ref):
    lane = lax.broadcasted_iota(jnp.int32, own_ref.shape[1:], 1)

    def several(group, unused):
        for member in range(4):
            pair = 4 * group + member
            other = jnp.where(lane < sensors, decoded(code_ref[pair], sensors), 0.0)
            merged_ref[pair] = coded_with_grade(own_ref[pair] + other, sensors)
        return unused

    lax.fori_loop(0, own_ref.shape[0] // 4, several, 0)


def merge(own, code, sensors):
    return pl.pallas_call(
        functools.partial(merge_kernel, sensors),
        out_shape=jax.ShapeDtypeStruct(code.shape, code.dtype),
        in_specs=[pl.BlockSpec(memory_space=pltpu.VMEM)] * 2,
        out_specs=pl.BlockSpec(memory_space=pltpu.VMEM),
        name="merge",
        compiler_params=pltpu.CompilerParams(vmem_limit_bytes=4 << 20),
    )(own, code)


def decode_kernel(own_ref, other_ref, out_ref):
    sensors = out_ref.shape[3]
    core = lax.rem(lax.axis_index("param"), 2)

    def one(pair, unused):
        out_ref[pair, core] = decoded(own_ref[pair], sensors)[:, :sensors]
        out_ref[pair, 1 - core] = decoded(other_ref[pair], sensors)[:, :sensors]
        return unused

    lax.fori_loop(0, own_ref.shape[0], one, 0, unroll=4)


def decode(own, other, sensors):
    pairs, steps, unused = own.shape
    out = pl.pallas_call(
        decode_kernel,
        out_shape=jax.ShapeDtypeStruct((pairs, 2, steps, sensors), jnp.float32),
        in_specs=[pl.BlockSpec(memory_space=pltpu.VMEM)] * 2,
        out_specs=pl.BlockSpec(memory_space=pltpu.VMEM),
        name="decode",
        compiler_params=pltpu.CompilerParams(vmem_limit_bytes=6 << 20),
    )(own, other)
    return out.reshape(2 * pairs, steps, sensors)


def forcing_kernel(place_ref, code_ref, observed_ref, diag_ref, forcing_ref):
    sensors = diag_ref.shape[0]
    copies, steps, unused, width = forcing_ref.shape
    total = None
    for part in range(code_ref.shape[0]):
        code = code_ref[part].astype(jnp.int32).astype(jnp.float32)
        term = code * scale_of(code[:, sensors : sensors + 1])
        total = term if total is None else total + term
    misfit = observed_ref[0].astype(jnp.float32) - total[:, :sensors]
    rows = lax.dot_general(
        misfit,
        diag_ref[...],
        (((1,), (1,)), ((), ())),
        precision=lax.Precision.HIGHEST,
        preferred_element_type=jnp.float32,
    )
    rows = jnp.concatenate([rows, jnp.zeros((steps, width - sensors), jnp.float32)], axis=1)
    for copy in range(copies):
        for step in range(steps):
            forcing_ref[copy, step] = rows[step : step + 1]


def force(code, observed, diag_inverse, place, copies, width):
    parts, steps, wide = code.shape
    sensors = diag_inverse.shape[0]
    return pl.pallas_call(
        forcing_kernel,
        out_shape=jax.ShapeDtypeStruct((copies, steps, 1, width), jnp.float32),
        grid_spec=pltpu.PrefetchScalarGridSpec(
            num_scalar_prefetch=1,
            grid=(1,),
            in_specs=[
                pl.BlockSpec((parts, steps, wide), lambda i, place: (0, 0, 0)),
                pl.BlockSpec((1, steps, sensors), lambda i, place: (place[0], 0, 0)),
                pl.BlockSpec((sensors, sensors), lambda i, place: (0, 0)),
            ],
            out_specs=pl.BlockSpec((copies, steps, 1, width), lambda i, place: (0, 0, 0, 0)),
        ),
        name="forcing",
    )(place, code, observed, diag_inverse)


def per_device(params, kernel, lag_offsets, observed, diag_inverse, coupling):
    samples, step_count, col_count = params.shape
    lag_count, unused_cols, sensors = kernel.shape
    width = -(-sensors // LANES) * LANES
    group = lax.axis_size("param")
    share = samples // group
    by_step = jnp.swapaxes(params, 0, 1)
    rim = from_behind(by_step[step_count - (REACH - 1) :], "tm", 1)
    near = prepare_near(diag_inverse, coupling, width)
    rim, near = lax.optimization_barrier((rim, near))
    assert share == 1
    chips = [list(range(core, group, 2)) for core in range(2)]
    partner = [(i, i ^ 1) for i in range(group)]
    code, own = predict(
        jnp.concatenate([rim, by_step], axis=0), jnp.swapaxes(kernel, 1, 2), lag_offsets
    )
    code = merge(own, lax.ppermute(code, "param", partner), sensors)
    place = lax.axis_index("param").astype(jnp.int32).reshape(1)
    code, place = lax.optimization_barrier((code, place))
    code = lax.all_to_all(code, "param", 0, 0, tiled=True, axis_index_groups=chips)
    blocks = lax.axis_size("tm")
    forced = force(code, observed, diag_inverse, place, blocks, width)
    forced, coupling = lax.optimization_barrier((forced, coupling))
    every = lax.all_to_all(forced, "tm", 0, 0, tiled=True)
    factors = (*near, *prepare_far(diag_inverse, coupling, width))
    code = run_chain(step_count, group // 2, *factors, every.reshape(-1, 1, width))
    code = lax.all_to_all(code, "param", 0, 0, tiled=True, axis_index_groups=chips)
    return decode(code, lax.ppermute(code, "param", partner), sensors)


def solution(mesh):
    in_specs = (P(None, "tm", "param"), P(None, "param", None), P(), P(None, "tm", None), P(), P())
    out_specs = P(None, "tm", None)
    return jax.shard_map(
        per_device, mesh=mesh, in_specs=in_specs, out_specs=out_specs, check_vma=False
    )
```

```python
import functools

import jax
import jax.numpy as jnp
from jax import lax
from jax.experimental import pallas as pl
from jax.experimental.pallas import tpu as pltpu
from jax.sharding import PartitionSpec as P

REACH = 12
AHEAD = 3
LANES = 128
LEVELS = 32700.0
OCTAVE = 64.0
TINY = 1e-37


def from_behind(block, axis, distance):
    devices = range(lax.axis_size(axis))
    route = [(i - distance, i) for i in devices if i - distance in devices]
    return lax.ppermute(block, axis, route)


def grade_of(rows):
    largest = jnp.maximum(jnp.max(jnp.abs(rows), axis=-1, keepdims=True), TINY)
    return jnp.ceil(jnp.log2(largest) * OCTAVE)


def coded(rows, grade):
    return jnp.round(rows * (LEVELS * jnp.exp2(grade * (-1.0 / OCTAVE))))


def scale_of(grade):
    return jnp.exp2(grade * (1.0 / OCTAVE)) * (1.0 / LEVELS)


def coded_with_grade(rows, place):
    grade = grade_of(rows)
    lane = lax.broadcasted_iota(jnp.int32, rows.shape, 1)
    code = jnp.where(lane == place, grade, coded(rows, grade))
    return code.astype(jnp.int32).astype(jnp.int16)


def row_chunks(rows):
    return [(start, min(LANES, rows - start)) for start in range(0, rows, LANES)]


def chain_kernel(
    block, sensors, near_ref, two_hi, two_lo, three_hi, three_lo, forcing_ref,
    code_ref, solved_ref, later_ref, carry_ref, even_ref, odd_ref, far_ref,
):
    width = near_ref.shape[2]
    pieces = list(range(width // LANES))
    reach = two_hi.shape[0]
    rest = [c for c in pieces if c * LANES >= reach]
    for ref in (later_ref, carry_ref, even_ref, odd_ref):
        ref[...] = jnp.zeros_like(ref)
    dot = functools.partial(jnp.dot, preferred_element_type=jnp.float32)

    def lanes(piece):
        return slice(piece * LANES, (piece + 1) * LANES)

    def wide(row):
        return jnp.broadcast_to(row, (8, LANES))

    def pair(turn, unused):
        diagonal = lax.broadcasted_iota(jnp.int32, (LANES, LANES), 0) == lax.broadcasted_iota(
            jnp.int32, (LANES, LANES), 1
        )
        row_id = lax.broadcasted_iota(jnp.int32, (16, LANES), 0)
        split = []
        for c in pieces:
            older = jnp.concatenate([even_ref[:, lanes(c)]] * 2, axis=0)
            newer = jnp.concatenate([odd_ref[:, lanes(c)]] * 2, axis=0)
            both = jnp.where(row_id < 2, older, jnp.where(row_id < 4, newer, 0.0))
            high = both.astype(jnp.bfloat16).astype(jnp.float32)
            split.append(
                jnp.where((row_id == 0) | (row_id == 2), high, both - high).astype(jnp.bfloat16)
            )
        operand = jnp.concatenate(split, axis=1)
        front = operand[:, :reach]
        far_ref[0] = dot(front, two_hi[...]) + dot(front, two_lo[...])
        far_ref[1] = dot(operand, three_hi[...]) + dot(operand, three_lo[...])

        for half in range(2):
            t = 2 * turn + half
            prev_ref, new_ref = ((odd_ref, even_ref), (even_ref, odd_ref))[half]
            behind = [prev_ref[:, lanes(c)] for c in pieces]
            for piece, (start, rows) in enumerate(row_chunks(sensors)):
                sums = []
                for row in range(start, start + rows, 8):
                    total = later_ref[row : row + 8, :]
                    for c in pieces:
                        total = total + near_ref[0, row : row + 8, lanes(c)] * behind[c]
                    sums.append(total)
                column = jnp.sum(jnp.concatenate(sums, axis=0), axis=1, keepdims=True)
                line = jnp.sum(jnp.where(diagonal[:rows], column, 0.0), axis=0, keepdims=True)
                base = wide(forcing_ref[t, :, lanes(piece)])
                if half == 0:
                    base = base + wide(carry_ref[0:1, lanes(piece)])
                else:
                    base = base + (
                        wide(far_ref[1, 0:1, lanes(piece)]) + wide(far_ref[1, 1:2, lanes(piece)])
                    )
                base = base + (
                    wide(far_ref[0, 2 * half : 2 * half + 1, lanes(piece)])
                    + wide(far_ref[0, 2 * half + 1 : 2 * half + 2, lanes(piece)])
                )
                solved = wide(line) + base
                new_ref[:, lanes(piece)] = solved
                solved_ref[lax.rem(t, block), :, lanes(piece)] = solved[0:1]
            gate = jnp.minimum(jnp.abs(sums[-1]), 0.0)
            behind = {c: prev_ref[:, lanes(c)] + gate for c in rest}
            for start in range(0, sensors, 8):
                total = None
                for c in rest:
                    term = near_ref[1, start : start + 8, lanes(c)] * behind[c]
                    total = term if total is None else total + term
                later_ref[start : start + 8, :] = total
        carry_ref[0:1, :] = far_ref[1, 2:3] + far_ref[1, 3:4]
        return unused

    turns = (lax.axis_index("tm") + 1) * (block // 2)
    def several(group, unused):
        for member in range(8):
            unused = pair(8 * group + member, unused)
        return unused

    lax.fori_loop(0, turns // 8, several, 0)
    own = jnp.concatenate([solved_ref[row] for row in range(block)], axis=0)
    code = coded_with_grade(own, sensors)
    for copy in range(code_ref.shape[0]):
        code_ref[copy] = code


def run_chain(block, copies, near, two_hi, two_lo, three_hi, three_lo, forcing):
    unused_lags, sensors, width = near.shape
    steps = forcing.shape[0]
    code, unused_rows = pl.pallas_call(
        functools.partial(chain_kernel, block, sensors),
        out_shape=(
            jax.ShapeDtypeStruct((copies, block, width), jnp.int16),
            jax.ShapeDtypeStruct((block, 1, width), jnp.float32),
        ),
        in_specs=[pl.BlockSpec(memory_space=pltpu.VMEM)] * 6,
        out_specs=[pl.BlockSpec(memory_space=pltpu.VMEM)] * 2,
        scratch_shapes=[
            pltpu.VMEM((sensors, LANES), jnp.float32),
            pltpu.VMEM((8, width), jnp.float32),
            pltpu.VMEM((8, width), jnp.float32),
            pltpu.VMEM((8, width), jnp.float32),
            pltpu.VMEM((2, 16, width), jnp.float32),
        ],
        name="chain",
    )(near, two_hi, two_lo, three_hi, three_lo, forcing)
    return code


def high_low(array):
    high = array.astype(jnp.bfloat16).astype(jnp.float32)
    return high.astype(jnp.bfloat16), (array - high).astype(jnp.bfloat16)


def factor(diag_ref, coupling_ref, lag):
    sensors = diag_ref.shape[0]
    lines = []
    for start in range(0, sensors, 2 * LANES):
        end = min(start + 2 * LANES, sensors)
        lines.append(
            -jnp.dot(
                diag_ref[start:end, :end],
                coupling_ref[lag, :end, :],
                precision=lax.Precision.HIGHEST,
                preferred_element_type=jnp.float32,
            )
        )
    return jnp.concatenate(lines, axis=0)


def turned(square_ref, high_ref, low_ref):
    for row in range(0, high_ref.shape[0], LANES):
        for column in range(0, high_ref.shape[1], LANES):
            tile = square_ref[column : column + LANES, row : row + LANES].T
            high, low = high_low(tile)
            high_ref[row : row + LANES, column : column + LANES] = high
            low_ref[row : row + LANES, column : column + LANES] = low


def near_kernel(diag_ref, coupling_ref, near_ref, high_ref, low_ref, square_ref):
    sensors = diag_ref.shape[0]
    near_ref[...] = jnp.zeros_like(near_ref)
    square_ref[...] = jnp.zeros_like(square_ref)
    near_ref[0, :, :sensors] = factor(diag_ref, coupling_ref, 0)
    second = factor(diag_ref, coupling_ref, 1)
    near_ref[1, :, :sensors] = second
    square_ref[:sensors, :sensors] = second
    turned(square_ref, high_ref, low_ref)


def far_kernel(diag_ref, coupling_ref, high_ref, low_ref, square_ref):
    sensors = diag_ref.shape[0]
    square_ref[...] = jnp.zeros_like(square_ref)
    square_ref[:sensors, :sensors] = factor(diag_ref, coupling_ref, 0)
    turned(square_ref, high_ref, low_ref)


def prepare_near(diag_inverse, coupling, width):
    sensors = diag_inverse.shape[0]
    part = jax.ShapeDtypeStruct((2 * LANES, width), jnp.bfloat16)
    return pl.pallas_call(
        near_kernel,
        out_shape=(jax.ShapeDtypeStruct((2, sensors, width), jnp.float32), part, part),
        in_specs=[
            pl.BlockSpec((sensors, sensors), lambda _: (0, 0)),
            pl.BlockSpec((2, sensors, sensors), lambda _: (0, 0, 0)),
        ],
        out_specs=[
            pl.BlockSpec((2, sensors, width), lambda _: (0, 0, 0)),
            pl.BlockSpec((2 * LANES, width), lambda _: (0, 0)),
            pl.BlockSpec((2 * LANES, width), lambda _: (0, 0)),
        ],
        grid=(1,),
        scratch_shapes=[pltpu.VMEM((width, width), jnp.float32)],
        cost_estimate=pl.CostEstimate(
            flops=12 * 2 * sensors**3, bytes_accessed=16 * sensors**2, transcendentals=0
        ),
        name="near_factors",
    )(diag_inverse, coupling)


def prepare_far(diag_inverse, coupling, width):
    sensors = diag_inverse.shape[0]
    part = jax.ShapeDtypeStruct((width, width), jnp.bfloat16)
    return pl.pallas_call(
        far_kernel,
        out_shape=(part, part),
        in_specs=[
            pl.BlockSpec((sensors, sensors), lambda _: (0, 0)),
            pl.BlockSpec((1, sensors, sensors), lambda _: (2, 0, 0)),
        ],
        out_specs=[pl.BlockSpec((width, width), lambda _: (0, 0))] * 2,
        grid=(1,),
        scratch_shapes=[pltpu.VMEM((width, width), jnp.float32)],
        cost_estimate=pl.CostEstimate(
            flops=12 * sensors**3, bytes_accessed=12 * sensors**2, transcendentals=0
        ),
        name="far_factors",
    )(diag_inverse, coupling)


def predict_kernel(
    offsets_ref, rim_hbm, steps_hbm, kernel_hbm, code_ref, own_ref,
    source_ref, kernel_ref, total_ref, arrived, here,
):
    samples, cols = source_ref.shape[1:]
    steps = code_ref.shape[1]
    lag_count, sensors, unused = kernel_ref.shape

    def fetch(lag):
        return pltpu.make_async_copy(kernel_hbm.at[lag], kernel_ref.at[lag], arrived.at[lag])

    rim_rows = rim_hbm.shape[0]
    inputs = [
        pltpu.make_async_copy(steps_hbm, source_ref.at[rim_rows:], here.at[0]),
        pltpu.make_async_copy(rim_hbm, source_ref.at[:rim_rows], here.at[1]),
    ]
    for copy in inputs:
        copy.start()
    for lag in range(AHEAD):
        fetch(lag).start()
    total_ref[...] = jnp.zeros_like(total_ref)
    for copy in inputs:
        copy.wait()

    def add(lag, unused):
        fetch(lag).wait()

        @pl.when(lag + AHEAD < lag_count)
        def more():
            fetch(lag + AHEAD).start()

        window = source_ref[pl.ds(REACH - 1 - offsets_ref[lag], steps)]
        window = window.reshape(steps * samples, cols)
        for start in range(0, sensors, 2 * LANES):
            end = min(start + 2 * LANES, sensors)
            product = lax.dot_general(
                window,
                kernel_ref[lag, start:end, :],
                (((1,), (1,)), ((), ())),
                preferred_element_type=jnp.float32,
            )
            for at in range(start, end, LANES):
                size = min(LANES, end - at)
                piece = product[:, at - start : at - start + size]
                total_ref[at // LANES, :, :size] = total_ref[at // LANES, :, :size] + piece
        return unused

    lax.fori_loop(0, lag_count, add, 0)

    core = lax.rem(lax.axis_index("param"), 2)

    def rows_of(sample):
        return jnp.concatenate(
            [
                total_ref[c, pl.ds(sample, steps, stride=samples), :]
                for c in range(total_ref.shape[0])
            ],
            axis=1,
        )

    def several(group, unused):
        for member in range(4):
            pair = 4 * group + member
            code_ref[pair] = coded_with_grade(rows_of(2 * pair + 1 - core), sensors)
            own_ref[pair] = rows_of(2 * pair + core)
        return unused

    lax.fori_loop(0, samples // 8, several, 0)


def predict(rim, by_step, kernel, lag_offsets):
    lag_count, sensors, cols = kernel.shape
    steps, samples, unused_cols = by_step.shape
    width = -(-sensors // LANES) * LANES
    return pl.pallas_call(
        predict_kernel,
        out_shape=(
            jax.ShapeDtypeStruct((samples // 2, steps, width), jnp.int16),
            jax.ShapeDtypeStruct((samples // 2, steps, width), jnp.float32),
        ),
        in_specs=[
            pl.BlockSpec(memory_space=pltpu.SMEM),
            pl.BlockSpec(memory_space=pl.ANY),
            pl.BlockSpec(memory_space=pl.ANY),
            pl.BlockSpec(memory_space=pl.ANY),
        ],
        out_specs=[pl.BlockSpec(memory_space=pltpu.VMEM)] * 2,
        scratch_shapes=[
            pltpu.VMEM((rim.shape[0] + steps, samples, cols), jnp.bfloat16),
            pltpu.VMEM((lag_count, sensors, cols), jnp.bfloat16),
            pltpu.VMEM((width // LANES, steps * samples, LANES), jnp.float32),
            pltpu.SemaphoreType.DMA((lag_count,)),
            pltpu.SemaphoreType.DMA((2,)),
        ],
        cost_estimate=pl.CostEstimate(
            flops=2 * steps * samples * lag_count * cols * sensors,
            bytes_accessed=2 * lag_count * cols * sensors,
            transcendentals=0,
        ),
        name="predict",
    )(lag_offsets, rim, by_step, kernel)


def decoded(code, sensors):
    values = code.astype(jnp.int32).astype(jnp.float32)
    return values * scale_of(values[:, sensors : sensors + 1])


def merge_kernel(sensors, own_ref, code_ref, merged_ref):
    lane = lax.broadcasted_iota(jnp.int32, own_ref.shape[1:], 1)

    def several(group, unused):
        for member in range(4):
            pair = 4 * group + member
            other = jnp.where(lane < sensors, decoded(code_ref[pair], sensors), 0.0)
            merged_ref[pair] = coded_with_grade(own_ref[pair] + other, sensors)
        return unused

    lax.fori_loop(0, own_ref.shape[0] // 4, several, 0)


def merge(own, code, sensors):
    return pl.pallas_call(
        functools.partial(merge_kernel, sensors),
        out_shape=jax.ShapeDtypeStruct(code.shape, code.dtype),
        in_specs=[pl.BlockSpec(memory_space=pltpu.VMEM)] * 2,
        out_specs=pl.BlockSpec(memory_space=pltpu.VMEM),
        name="merge",
        compiler_params=pltpu.CompilerParams(vmem_limit_bytes=4 << 20),
    )(own, code)


def decode_kernel(own_ref, other_ref, out_ref):
    sensors = out_ref.shape[3]
    core = lax.rem(lax.axis_index("param"), 2)

    def one(pair, unused):
        out_ref[pair, core] = decoded(own_ref[pair], sensors)[:, :sensors]
        out_ref[pair, 1 - core] = decoded(other_ref[pair], sensors)[:, :sensors]
        return unused

    lax.fori_loop(0, own_ref.shape[0], one, 0, unroll=4)


def decode(own, other, sensors):
    pairs, steps, unused = own.shape
    out = pl.pallas_call(
        decode_kernel,
        out_shape=jax.ShapeDtypeStruct((pairs, 2, steps, sensors), jnp.float32),
        in_specs=[pl.BlockSpec(memory_space=pltpu.VMEM)] * 2,
        out_specs=pl.BlockSpec(memory_space=pltpu.VMEM),
        name="decode",
        compiler_params=pltpu.CompilerParams(vmem_limit_bytes=6 << 20),
    )(own, other)
    return out.reshape(2 * pairs, steps, sensors)


def forcing_kernel(place_ref, code_ref, observed_ref, diag_ref, forcing_ref):
    sensors = diag_ref.shape[0]
    copies, steps, unused, width = forcing_ref.shape
    total = None
    for part in range(code_ref.shape[0]):
        code = code_ref[part].astype(jnp.int32).astype(jnp.float32)
        term = code * scale_of(code[:, sensors : sensors + 1])
        total = term if total is None else total + term
    misfit = observed_ref[0].astype(jnp.float32) - total[:, :sensors]
    rows = lax.dot_general(
        misfit,
        diag_ref[...],
        (((1,), (1,)), ((), ())),
        precision=lax.Precision.HIGHEST,
        preferred_element_type=jnp.float32,
    )
    rows = jnp.concatenate([rows, jnp.zeros((steps, width - sensors), jnp.float32)], axis=1)
    for copy in range(copies):
        for step in range(steps):
            forcing_ref[copy, step] = rows[step : step + 1]


def force(code, observed, diag_inverse, place, copies, width):
    parts, steps, wide = code.shape
    sensors = diag_inverse.shape[0]
    return pl.pallas_call(
        forcing_kernel,
        out_shape=jax.ShapeDtypeStruct((copies, steps, 1, width), jnp.float32),
        grid_spec=pltpu.PrefetchScalarGridSpec(
            num_scalar_prefetch=1,
            grid=(1,),
            in_specs=[
                pl.BlockSpec((parts, steps, wide), lambda i, place: (0, 0, 0)),
                pl.BlockSpec((1, steps, sensors), lambda i, place: (place[0], 0, 0)),
                pl.BlockSpec((sensors, sensors), lambda i, place: (0, 0)),
            ],
            out_specs=pl.BlockSpec((copies, steps, 1, width), lambda i, place: (0, 0, 0, 0)),
        ),
        name="forcing",
    )(place, code, observed, diag_inverse)


def per_device(params, kernel, lag_offsets, observed, diag_inverse, coupling):
    samples, step_count, col_count = params.shape
    lag_count, unused_cols, sensors = kernel.shape
    width = -(-sensors // LANES) * LANES
    group = lax.axis_size("param")
    share = samples // group
    by_step = jnp.swapaxes(params, 0, 1)
    rim = from_behind(by_step[step_count - (REACH - 1) :], "tm", 1)
    near = prepare_near(diag_inverse, coupling, width)
    rim, near = lax.optimization_barrier((rim, near))
    assert share == 1
    chips = [list(range(core, group, 2)) for core in range(2)]
    partner = [(i, i ^ 1) for i in range(group)]
    code, own = predict(rim, by_step, jnp.swapaxes(kernel, 1, 2), lag_offsets)
    code = merge(own, lax.ppermute(code, "param", partner), sensors)
    place = lax.axis_index("param").astype(jnp.int32).reshape(1)
    code, place = lax.optimization_barrier((code, place))
    code = lax.all_to_all(code, "param", 0, 0, tiled=True, axis_index_groups=chips)
    blocks = lax.axis_size("tm")
    forced = force(code, observed, diag_inverse, place, blocks, width)
    forced, coupling = lax.optimization_barrier((forced, coupling))
    every = lax.all_to_all(forced, "tm", 0, 0, tiled=True)
    factors = (*near, *prepare_far(diag_inverse, coupling, width))
    code = run_chain(step_count, group // 2, *factors, every.reshape(-1, 1, width))
    code = lax.all_to_all(code, "param", 0, 0, tiled=True, axis_index_groups=chips)
    return decode(code, lax.ppermute(code, "param", partner), sensors)


def solution(mesh):
    in_specs = (P(None, "tm", "param"), P(None, "param", None), P(), P(None, "tm", None), P(), P())
    out_specs = P(None, "tm", None)
    return jax.shard_map(
        per_device, mesh=mesh, in_specs=in_specs, out_specs=out_specs, check_vma=False
    )
```
